32 devices in a mesh: ctx: 8 (over y, x, core), exp: 4 (over z).
Axes of the slice: x: 2, y: 2, z: 4, core: 2. Of those that a mesh axis runs over, the one named last changes fastest.
Arguments:
- queries: bfloat16 [512, 64, 512], P('ctx', 'exp'), may hold values from -17 to 17
- latent: bfloat16 [512, 512], P('ctx'), may hold values from -2 to 2
- grad_out: bfloat16 [512, 64, 512], P('ctx', 'exp'), may hold values from -6 to 6
- doc_ids: int32 [512], P('ctx'), may hold values from 0 to 5, as said below
- tokens: bfloat16 [4096, 7168], P(('ctx', 'exp')), may hold values from -6 to 6
- token_grads: bfloat16 [4096, 7168], P(('ctx', 'exp')), may hold values from -1.5 to 1.5
- gate_values: float32 [4096, 8], P(('ctx', 'exp')), may hold values from 0.3 to 3
- expert_ids: int32 [4096, 8], P(('ctx', 'exp')), may hold values from 0 to 255, as said below
- gate_order: int32 [32, 128], P(('ctx', 'exp')), may hold values from 0 to 127, each once within a row
- w_gate: bfloat16 [4, 7168, 2048], P('exp', None, 'ctx'), may hold values from -0.0625 to 0.0625
- w_up: bfloat16 [4, 7168, 2048], P('exp', None, 'ctx'), may hold values from -0.0625 to 0.0625
- w_down: bfloat16 [4, 2048, 7168], P('exp', 'ctx'), may hold values from -0.125 to 0.125
Outputs:
- d_queries: bfloat16 [512, 64, 512], P('ctx', 'exp')
- d_latent: bfloat16 [512, 512], P('ctx')
- d_tokens: bfloat16 [4096, 7168], P(('ctx', 'exp'))
- d_gates: bfloat16 [4096, 8], P(('ctx', 'exp'))
The draws below stay inside these ranges and needn't reach their ends.
Inputs may be any that keep to these rules, and one draw needn't show every extreme that they name: `doc_ids`: never falling along the sequence; every number below 6 occurs. `expert_ids`: each row names 8 different experts. For every index of ctx some expert below 4 is named by 2 or more rows of every device at that index. `gate_order`: each row holds every number below 128 once.
All inputs are finite; a program needn't handle non-finite values.
Results may differ from the reference program's by a relative error of at most 0.02.
Values may be sent and summed in bfloat16 or wider, within the bound.
No kernel may reach another device: no remote copies, remote signals or barrier semaphores. Data moves between devices by JAX's collectives and lax.ppermute only.
A program may use at most 128 MiB of HBM per device.

```python
import math
import jax
import jax.numpy as jnp
from jax import lax

D = 7168
HID = 2048
EXPERTS = 256
TOPK = 8
HEADS = 64
LAT = 512
SCALE_DIM = 192
T_ATT = 64
T_MOE = 128
CAP = 2
EXP_DEV = 1
DOCS = 6
N_INFL = 4
SEQ = 512
TOKENS = 4096
N_CTX = 8
N_EXP = 4
DEVICES = 32


def latent_pairs(key):
    base_key = jax.random.fold_in(key, 7)
    first_key = jax.random.fold_in(base_key, 0)
    base_rows = jnp.clip(0.8 * jax.random.normal(first_key, (SEQ, LAT), jnp.float32), -2.0, 2.0)
    latent_rows = base_rows
    return latent_rows


def draw_latent(key, part):
    latent_rows = latent_pairs(key)
    return latent_rows.astype(jnp.bfloat16)


def draw_queries(key, part):
    own_key = jax.random.fold_in(key, 9)
    noise_key = jax.random.fold_in(own_key, 0)
    result = jnp.clip(jax.random.normal(noise_key, (SEQ, HEADS, LAT), jnp.float32), -5.0, 5.0)
    return result.astype(jnp.bfloat16)


def draw_doc_ids(key, part):
    base_key = jax.random.fold_in(key, 13)
    block_key, offset_key = jax.random.split(base_key, 2)
    chosen_blocks = jnp.sort(jax.random.permutation(block_key, N_CTX)[:DOCS - 1])
    offsets = jax.random.randint(offset_key, (DOCS - 1,), 1, T_ATT)
    bounds = (chosen_blocks * T_ATT + offsets).astype(jnp.int32)
    positions = jnp.arange(SEQ, dtype=jnp.int32)
    return jnp.sum((positions[:, None] >= bounds[None, :]).astype(jnp.int32), axis=1).astype(jnp.int32)


def draw_expert_ids(key, part):
    base_key = jax.random.fold_in(key, 11)
    noise_key, popular_key, forced_key, row_key = jax.random.split(base_key, 4)
    blocks = TOKENS // T_MOE
    jitter_values = jax.random.randint(noise_key, (TOKENS, EXPERTS), 0, 32768)
    favored_expert = jax.random.randint(popular_key, (EXPERTS,), 0, 6)
    favored_expert = favored_expert * favored_expert * 1024
    forced_expert = jax.random.randint(forced_key, (N_CTX,), 0, N_INFL)
    block_expert = jnp.repeat(forced_expert, N_EXP)
    row_scores = jax.random.randint(row_key, (blocks, T_MOE), 0, 1 << 20) * T_MOE + jnp.arange(T_MOE, dtype=jnp.int32)
    order_rank = jnp.argsort(jnp.argsort(row_scores, axis=1), axis=1)
    pinned_rows = (order_rank < CAP).reshape(TOKENS)
    expert_span = jnp.arange(EXPERTS, dtype=jnp.int32)
    row_target_expert = jnp.repeat(block_expert, T_MOE)
    favor_boost = jnp.where(pinned_rows[:, None] & (expert_span[None, :] == row_target_expert[:, None]), 1 << 30, 0)
    router_logits = (jitter_values + favored_expert[None, :]) * 256 + expert_span[None, :] + favor_boost
    ranked = jnp.argsort(-router_logits, axis=1)
    return ranked[:, :TOPK].astype(jnp.int32)


def block_scale(rng, extent, cuts, smallest, high):
    gain, own = 1.0, jax.random.fold_in(rng, 6)
    for axis_at, shards_of in cuts:
        steps = jnp.exp(jax.random.uniform(jax.random.fold_in(own, axis_at), (shards_of,), jnp.float32, smallest / len(cuts), high / len(cuts)))
        gain = gain * jnp.repeat(steps, extent[axis_at] // shards_of).reshape([-1 if axis == axis_at else 1 for axis in range(len(extent))])
    return gain


def normal_values(key, extent, deviation, reach, cuts=(), kind=jnp.bfloat16):
    drawn = jax.random.normal(key, extent, jnp.float32) * deviation
    if len(cuts) > 0:
        drawn = block_scale(key, extent, cuts, -0.22, 0.18) * drawn
    return jnp.clip(drawn, min=-reach, max=reach).astype(kind)


def setup_inputs(seed: int = 0) -> dict:
    key_list = jax.random.split(jax.random.key(seed), 13)
    queries = draw_queries(jax.random.fold_in(key_list[12], 71), 0)
    latent = draw_latent(jax.random.fold_in(key_list[12], 71), 0)
    grad_out = normal_values(key_list[2], (SEQ, HEADS, LAT), 1.0, 6.0, ((0, 8), (1, 4)))
    doc_ids = draw_doc_ids(jax.random.fold_in(key_list[12], 71), 0)
    tokens = normal_values(key_list[4], (TOKENS, D), 1.0, 6.0, ((0, 32),))
    token_grads = normal_values(key_list[5], (TOKENS, D), 0.25, 1.5, ((0, 32),))
    gate_values = jnp.clip(jnp.exp(math.log(3.0) - 2.3025851 * jax.random.uniform(key_list[6], (TOKENS, TOPK), jnp.float32) ** block_scale(key_list[6], (TOKENS, TOPK), ((0, 32),), -0.2, 0.2)), 0.3, 3.0)
    expert_ids = draw_expert_ids(jax.random.fold_in(key_list[12], 71), 0)
    gate_order = jax.vmap(lambda own: jax.random.permutation(own, T_MOE))(jax.random.split(key_list[8], DEVICES)).reshape((DEVICES, T_MOE)).astype(jnp.int32)
    w_gate = normal_values(key_list[9], (N_INFL, D, HID), D ** -0.5, 0.0625, ((0, 4), (2, 8)))
    w_up = normal_values(key_list[10], (N_INFL, D, HID), D ** -0.5, 0.0625, ((0, 4), (2, 8)))
    w_down = normal_values(key_list[11], (N_INFL, HID, D), HID ** -0.5, 0.125, ((0, 4), (1, 8)))
    return dict(queries=queries, latent=latent, grad_out=grad_out, doc_ids=doc_ids, tokens=tokens, token_grads=token_grads, gate_values=gate_values, expert_ids=expert_ids, gate_order=gate_order, w_gate=w_gate, w_up=w_up, w_down=w_down)


def attention_grads(queries, latent, grad_out, doc_ids):
    softmax_scale = SCALE_DIM ** -0.5
    allowed = doc_ids[None, :] == doc_ids[:, None]

    def one_head(carried, head_data):
        query_head, grad_head = head_data
        router_logits = softmax_scale * jnp.dot(query_head, latent.T, preferred_element_type=jnp.float32)
        router_logits = jnp.where(allowed, router_logits, -1e30)
        row_max = jnp.max(router_logits, axis=1, keepdims=True)
        unnorm = jnp.exp(router_logits - row_max)
        row_sum = jnp.sum(unnorm, axis=1, keepdims=True)
        output = jnp.dot(unnorm.astype(jnp.bfloat16), latent, preferred_element_type=jnp.float32) / row_sum
        log_sum = row_max + jnp.log(row_sum)
        delta_rows = jnp.sum(grad_head.astype(jnp.float32) * output, axis=1, keepdims=True)
        probs = jnp.exp(router_logits - log_sum)
        prob_grad = jnp.dot(grad_head, latent.T, preferred_element_type=jnp.float32)
        score_grad = (probs * (prob_grad - delta_rows)).astype(jnp.bfloat16)
        prob_weights = probs.astype(jnp.bfloat16)
        query_grad = softmax_scale * jnp.dot(score_grad, latent, preferred_element_type=jnp.float32)
        latent_grad = softmax_scale * jnp.dot(score_grad.T, query_head, preferred_element_type=jnp.float32)
        latent_grad = latent_grad + jnp.dot(prob_weights.T, grad_head, preferred_element_type=jnp.float32)
        return carried + latent_grad, query_grad.astype(jnp.bfloat16)

    heads_first = (jnp.transpose(queries, (1, 0, 2)), jnp.transpose(grad_out, (1, 0, 2)))
    latent_total, query_grads = lax.scan(one_head, jnp.zeros(latent.shape, jnp.float32), heads_first)
    return jnp.transpose(query_grads, (1, 0, 2)), latent_total.astype(jnp.bfloat16)


def expert_grads(tokens, token_grads, gate_values, expert_ids, gate_order, w_gate, w_up, w_down):
    blocks = gate_order.shape[0]
    block_rows = gate_order.shape[1]
    resident = N_EXP * EXP_DEV
    model_width = tokens.shape[1]
    shard = HID // N_CTX
    ids_blocks = expert_ids.reshape(blocks, block_rows, TOPK)
    expert_span = jnp.arange(resident, dtype=jnp.int32)
    matches = (ids_blocks[:, :, :, None] == expert_span).astype(jnp.int32)
    hits = jnp.sum(matches, axis=2)
    earlier = (gate_order[:, :, None] < gate_order[:, None, :]).astype(jnp.int32)
    ranks = jnp.einsum("but,bue->bte", earlier, hits)
    chosen = (hits[:, :, :, None] == 1) & (ranks[:, :, :, None] == jnp.arange(CAP, dtype=jnp.int32))
    chosen_int = chosen.astype(jnp.int32)
    row_index = jnp.einsum("btes,t->bes", chosen_int, jnp.arange(block_rows, dtype=jnp.int32))
    filled = jnp.sum(chosen_int, axis=1)
    block_index = jnp.arange(blocks, dtype=jnp.int32)[:, None, None]
    fill_mask = filled.astype(jnp.bfloat16)[:, :, :, None]
    picked_in = tokens.reshape(blocks, block_rows, model_width)[block_index, row_index] * fill_mask
    picked_grad = token_grads.reshape(blocks, block_rows, model_width)[block_index, row_index] * fill_mask
    rows_in = jnp.transpose(picked_in, (1, 0, 2, 3)).reshape(resident, blocks * CAP, model_width)
    rows_grad = jnp.transpose(picked_grad, (1, 0, 2, 3)).reshape(resident, blocks * CAP, model_width)

    def one_expert(expert_data):
        expert_in, expert_grad, gate_mat, up_mat, down_mat = expert_data
        gate_pre = jnp.dot(expert_in, gate_mat, preferred_element_type=jnp.float32)
        up_pre = jnp.dot(expert_in, up_mat, preferred_element_type=jnp.float32)
        act_grad = jnp.dot(expert_grad, down_mat.T, preferred_element_type=jnp.float32)
        gate_sig = jax.nn.sigmoid(gate_pre)
        silu_val = gate_pre * gate_sig
        hidden_act = (silu_val * up_pre).astype(jnp.bfloat16)
        expert_score = jnp.sum(hidden_act.astype(jnp.float32) * act_grad, axis=1)
        gate_grad = (act_grad * up_pre * gate_sig * (1.0 + gate_pre * (1.0 - gate_sig))).astype(jnp.bfloat16)
        up_grad = (act_grad * silu_val).astype(jnp.bfloat16)
        rows_total = gate_grad.shape[0]
        gate_parts = gate_grad.reshape(rows_total, N_CTX, shard).astype(jnp.float32)
        up_parts = up_grad.reshape(rows_total, N_CTX, shard).astype(jnp.float32)
        gate_tiles = gate_mat.reshape(model_width, N_CTX, shard).astype(jnp.float32)
        up_tiles = up_mat.reshape(model_width, N_CTX, shard).astype(jnp.float32)
        parts = jnp.einsum("rch,dch->rcd", gate_parts, gate_tiles, precision=lax.Precision.HIGHEST)
        parts = parts + jnp.einsum("rch,dch->rcd", up_parts, up_tiles, precision=lax.Precision.HIGHEST)
        rounded = lax.optimization_barrier(parts.astype(jnp.bfloat16))
        expert_input = jnp.sum(rounded.astype(jnp.float32), axis=1).astype(jnp.bfloat16)
        return expert_input, expert_score.astype(jnp.bfloat16)

    expert_inputs, expert_scores = lax.map(one_expert, (rows_in, rows_grad, w_gate, w_up, w_down))
    back_rows = jnp.transpose(expert_inputs.reshape(resident, blocks, CAP, model_width), (1, 0, 2, 3))
    back_scores = jnp.transpose(expert_scores.reshape(resident, blocks, CAP), (1, 0, 2))
    gate_blocks = gate_values.reshape(blocks, block_rows, TOPK)
    gate_mass = jnp.sum(matches.astype(jnp.float32) * gate_blocks[:, :, :, None], axis=2)
    weighting = chosen.astype(jnp.float32) * gate_mass[:, :, :, None]
    d_tokens = jnp.einsum("btes,besd->btd", weighting, back_rows.astype(jnp.float32), precision=lax.Precision.HIGHEST)
    kept_scores = jnp.einsum("btes,bes->bte", chosen.astype(jnp.float32), back_scores.astype(jnp.float32), precision=lax.Precision.HIGHEST)
    d_gates = jnp.einsum("btke,bte->btk", matches.astype(jnp.float32), kept_scores, precision=lax.Precision.HIGHEST)
    return d_tokens.reshape(blocks * block_rows, model_width).astype(jnp.bfloat16), d_gates.reshape(blocks * block_rows, TOPK).astype(jnp.bfloat16)


def reference(queries, latent, grad_out, doc_ids, tokens, token_grads, gate_values, expert_ids, gate_order, w_gate, w_up, w_down):
    d_queries, d_latent = attention_grads(queries, latent, grad_out, doc_ids)
    d_tokens, d_gates = expert_grads(tokens, token_grads, gate_values, expert_ids, gate_order, w_gate, w_up, w_down)
    return (d_queries, d_latent, d_tokens, d_gates)
```

```python
import functools

import jax
import jax.numpy as jnp
from jax import lax
from jax.experimental import pallas as pl
from jax.experimental.pallas import tpu as pltpu
from jax.sharding import PartitionSpec as P

SCALE_DIM = 192
CAP = 2
LANES = 128
MIB = 1 << 20
F32 = jnp.float32
BF16 = jnp.bfloat16


def exchange(array, axis, mask):
    count = lax.axis_size(axis)
    return lax.ppermute(array, axis, [(i, i ^ mask) for i in range(count)])


def vmem_spec():
    return pl.BlockSpec(memory_space=pltpu.VMEM)


def any_spec():
    return pl.BlockSpec(memory_space=pl.ANY)


def nbytes(shape, dtype):
    total = jnp.dtype(dtype).itemsize
    for size in shape:
        total *= size
    return total


def call(body, name, outs, args, in_specs, scratch, limit, flops=0):
    moved = sum(nbytes(a.shape, a.dtype) for a in args)
    moved += sum(nbytes(o.shape, o.dtype) for o in outs)
    return pl.pallas_call(
        body,
        out_shape=outs,
        in_specs=in_specs,
        out_specs=[vmem_spec() for _ in outs],
        scratch_shapes=scratch,
        compiler_params=pltpu.CompilerParams(vmem_limit_bytes=limit),
        cost_estimate=pl.CostEstimate(flops=flops, bytes_accessed=moved, transcendentals=0),
        name=name,
    )(*args)


def route_body(n_exp, ids_ref, order_ref, gates_ref, tok_hbm, grad_hbm, *rest):
    msgs = rest[:n_exp]
    weight_ref, chosen_ref, held, sems = rest[n_exp:]
    copies = [
        pltpu.make_async_copy(src, held.at[i], sems.at[i])
        for i, src in enumerate((tok_hbm, grad_hbm))
    ]
    for copy in copies:
        copy.start()
    rows, top = ids_ref.shape
    slots = n_exp * CAP
    lane = lax.broadcasted_iota(jnp.int32, (rows, LANES), 1)
    expert = jnp.where(lane < slots, (lane >> (CAP.bit_length() - 1)) ^ lax.axis_index("exp"), -1)
    ids = ids_ref[...]
    gates = gates_ref[...]
    hits = jnp.zeros((rows, LANES), F32)
    mass = jnp.zeros((rows, LANES), F32)
    for j in range(top):
        match = ids[:, j : j + 1] == expert
        hits = hits + jnp.where(match, 1.0, 0.0)
        mass = mass + jnp.where(match, gates[:, j : j + 1], 0.0)
    order = jnp.broadcast_to(order_ref[...].astype(F32), (rows, rows))
    earlier = jnp.where(order < order.T, 1.0, 0.0).astype(BF16)
    ranks = jnp.dot(earlier, hits.astype(BF16), preferred_element_type=F32)
    slot = (lane & (CAP - 1)).astype(F32)
    chosen = jnp.where((hits == 1.0) & (ranks == slot), 1.0, 0.0)
    weight_ref[...] = chosen * mass
    chosen_ref[...] = chosen
    pick = chosen.T[:slots].astype(BF16)
    width = held.shape[2]
    step = width // 4
    for copy in copies:
        copy.wait()
    for c in range(4):
        cols = pl.ds(c * step, step)
        tok = jnp.dot(pick, held[0, :, cols], preferred_element_type=F32)
        grad = jnp.dot(pick, held[1, :, cols], preferred_element_type=F32)
        for k in range(n_exp):
            span = slice(k * CAP, (k + 1) * CAP)
            msgs[k][:, cols] = jnp.concatenate([tok[span], grad[span]], axis=0).astype(BF16)


def route(expert_ids, gate_order, gate_values, tokens, token_grads, n_exp):
    rows, width = tokens.shape
    outs = [jax.ShapeDtypeStruct((2 * CAP, width), BF16) for _ in range(n_exp)]
    outs += [jax.ShapeDtypeStruct((rows, LANES), F32)] * 2
    res = call(
        functools.partial(route_body, n_exp),
        "route",
        outs,
        (expert_ids, gate_order, gate_values, tokens, token_grads),
        [vmem_spec()] * 3 + [any_spec()] * 2,
        [pltpu.VMEM((2, rows, width), BF16), pltpu.SemaphoreType.DMA((2,))],
        12 * MIB,
        flops=4 * n_exp * CAP * rows * width,
    )
    return res[:n_exp], res[n_exp], res[n_exp + 1]


def attention_body(n_ctx, heads, row_block, *refs):
    q_ref, go_ref = refs[:2]
    blocks = refs[2 : 2 + n_ctx]
    dq_ref, even_ref, odd_ref = refs[2 + n_ctx : 5 + n_ctx]
    lat, keydoc, acc = refs[5 + n_ctx :]
    step = pl.program_id(0)
    per = blocks[0].shape[0]
    width = q_ref.shape[1]
    order = list(range(0, n_ctx, 2)) + list(range(1, n_ctx, 2))
    scale = SCALE_DIM ** (-0.5)

    @pl.when(step == 0)
    def _():
        for i, j in enumerate(order):
            lat[i * per : (i + 1) * per, :] = blocks[j][:, :width]
            keydoc[i * per : (i + 1) * per, :] = blocks[j][:, width:].astype(F32)
        acc[...] = jnp.zeros_like(acc)

    q = q_ref[...]
    go = go_ref[...]
    keys = lat[...]
    nt = (((1,), (1,)), ((), ()))
    tn = (((0,), (0,)), ((), ()))
    owner = lax.broadcasted_iota(jnp.int32, (per, row_block), 0)
    col = lax.broadcasted_iota(jnp.int32, (per, row_block), 1) + step * row_block
    spread = jnp.where((col >= owner * heads) & (col < (owner + 1) * heads), 1.0, 0.0).astype(BF16)
    qdoc = lax.dot_general(blocks[0][:, width:], spread, tn, preferred_element_type=F32)[:1]
    scores = lax.dot_general(keys, q, nt, preferred_element_type=F32) * scale
    reps = row_block // LANES
    kd = keydoc[...]
    kd = jnp.concatenate([kd] * reps, axis=1) if reps > 1 else kd
    scores = jnp.where(kd == qdoc, scores, -1e30)
    top = jnp.max(scores, axis=0, keepdims=True)
    probs = jnp.exp(scores - top)
    total = jnp.sum(probs, axis=0, keepdims=True)
    probs = probs * (1.0 / total)
    pgrad = lax.dot_general(keys, go, nt, preferred_element_type=F32)
    delta = jnp.sum(probs * pgrad, axis=0, keepdims=True)
    sgrad = (probs * (pgrad - delta)).astype(BF16)
    probs = probs.astype(BF16)
    dq = lax.dot_general(sgrad, keys, tn, preferred_element_type=F32) * scale
    dq_ref[...] = dq.astype(BF16)
    term = jnp.dot(sgrad, q, preferred_element_type=F32) * scale
    acc[...] += term + jnp.dot(probs, go, preferred_element_type=F32)

    @pl.when(step == pl.num_programs(0) - 1)
    def _():
        half = even_ref.shape[0]
        even_ref[...] = acc[:half, :].astype(BF16)
        odd_ref[...] = acc[half:, :].astype(BF16)


def attention(queries, grad_out, blocks):
    n_ctx = len(blocks)
    q_rows, heads, width = queries.shape
    rows = q_rows * heads
    keys = blocks[0].shape[0] * n_ctx
    row_block = min(256, rows)
    q = queries.reshape(rows, width)
    go = grad_out.reshape(rows, width)
    row_spec = pl.BlockSpec((row_block, width), lambda i: (i, 0))
    whole = lambda shape: pl.BlockSpec(shape, lambda i: (0, 0))
    half = (keys // 2, width)
    res = pl.pallas_call(
        functools.partial(attention_body, n_ctx, heads, row_block),
        grid=(rows // row_block,),
        in_specs=[row_spec, row_spec] + [whole(b.shape) for b in blocks],
        out_specs=[row_spec, whole(half), whole(half)],
        out_shape=[
            jax.ShapeDtypeStruct((rows, width), BF16),
            jax.ShapeDtypeStruct(half, BF16),
            jax.ShapeDtypeStruct(half, BF16),
        ],
        scratch_shapes=[
            pltpu.VMEM((keys, width), BF16),
            pltpu.VMEM((keys, LANES), F32),
            pltpu.VMEM((keys, width), F32),
        ],
        compiler_params=pltpu.CompilerParams(vmem_limit_bytes=20 * MIB),
        cost_estimate=pl.CostEstimate(
            flops=10 * rows * keys * width, bytes_accessed=6 * rows * width, transcendentals=0
        ),
        name="attention",
    )(q, go, *blocks)
    return res[0].reshape(queries.shape), res[1], res[2]


def split_score(total, lane):
    high = total.astype(BF16).astype(F32)
    low = total - high
    return jnp.where(lane == 0, high, jnp.where(lane == 1, low, 0.0)).astype(BF16)


def expert_body(n_ctx, chunks, *refs):
    blocks = refs[:n_ctx]
    wg_hbm, wu_hbm, wd_hbm, even_ref, odd_ref = refs[n_ctx : n_ctx + 5]
    xt, xg, wg, wu, wd, sems = refs[n_ctx + 5 :]
    width, hid = wg.shape
    step = width // chunks
    copies = {}
    for i, (src, dst) in enumerate(((wg_hbm, wg), (wu_hbm, wu), (wd_hbm, wd))):
        for c in range(chunks):
            cols = pl.ds(c * step, step)
            if i < 2:
                copy = pltpu.make_async_copy(src.at[0, cols, :], dst.at[cols, :], sems.at[i, c])
            else:
                copy = pltpu.make_async_copy(src.at[0, :, cols], dst.at[:, cols], sems.at[i, c])
            copies[i, c] = copy
    for i in range(3):
        for c in range(chunks):
            copies[i, c].start()
    order = list(range(0, n_ctx, 2)) + list(range(1, n_ctx, 2))
    per = blocks[0].shape[0] // 2
    for i, j in enumerate(order):
        xt[i * per : (i + 1) * per, :] = blocks[j][:per, :]
        xg[i * per : (i + 1) * per, :] = blocks[j][per:, :]
    rows = per * n_ctx
    nt = (((1,), (1,)), ((), ()))
    gate = jnp.zeros((rows, hid), F32)
    up = jnp.zeros((rows, hid), F32)
    act = jnp.zeros((rows, hid), F32)
    for c in range(chunks):
        cols = pl.ds(c * step, step)
        copies[0, c].wait()
        gate = gate + jnp.dot(xt[:, cols], wg[cols, :], preferred_element_type=F32)
    for c in range(chunks):
        cols = pl.ds(c * step, step)
        copies[1, c].wait()
        up = up + jnp.dot(xt[:, cols], wu[cols, :], preferred_element_type=F32)
    for c in range(chunks):
        cols = pl.ds(c * step, step)
        copies[2, c].wait()
        act = act + lax.dot_general(xg[:, cols], wd[:, cols], nt, preferred_element_type=F32)
    sig = jax.nn.sigmoid(gate)
    silu = gate * sig
    hidden = (silu * up).astype(BF16).astype(F32)
    score = jnp.sum(hidden * act, axis=1, keepdims=True)
    ggrad = (act * up * sig * (1.0 + gate * (1.0 - sig))).astype(BF16)
    ugrad = (act * silu).astype(BF16)
    half = rows // 2
    lane = lax.broadcasted_iota(jnp.int32, (rows, LANES), 1)
    tail = split_score(score, lane)
    even_ref[:, pl.ds(width, LANES)] = tail[:half]
    odd_ref[:, pl.ds(width, LANES)] = tail[half:]
    fine = 512
    for c in range(width // fine):
        cols = pl.ds(c * fine, fine)
        part = lax.dot_general(ggrad, wg[cols, :], nt, preferred_element_type=F32)
        part = part + lax.dot_general(ugrad, wu[cols, :], nt, preferred_element_type=F32)
        part = part.astype(BF16)
        even_ref[:, cols] = part[:half]
        odd_ref[:, cols] = part[half:]


def experts(blocks, w_gate, w_up, w_down):
    n_ctx = len(blocks)
    width = blocks[0].shape[1]
    hid = w_gate.shape[2]
    rows = blocks[0].shape[0] // 2 * n_ctx
    chunks = 4
    out = jax.ShapeDtypeStruct((rows // 2, width + LANES), BF16)
    return call(
        functools.partial(expert_body, n_ctx, chunks),
        "experts",
        [out, out],
        (*blocks, w_gate, w_up, w_down),
        [vmem_spec()] * n_ctx + [any_spec()] * 3,
        [
            pltpu.VMEM((rows, width), BF16),
            pltpu.VMEM((rows, width), BF16),
            pltpu.VMEM((width, hid), BF16),
            pltpu.VMEM((width, hid), BF16),
            pltpu.VMEM((hid, width), BF16),
            pltpu.SemaphoreType.DMA((3, chunks)),
        ],
        min(56 * MIB, 14 * MIB + 12 * nbytes((rows, width), BF16)),
        flops=10 * rows * width * hid,
    )


def pair_body(n_out, keep_ref, got_ref, *outs):
    width = outs[0].shape[1] - LANES
    per = outs[0].shape[0]
    for i in range(n_out):
        span = pl.ds(i * per, per)
        total = keep_ref[span, :].astype(F32) + got_ref[span, :].astype(F32)
        outs[i][:, :width] = total[:, :width].astype(BF16)
        lane = lax.broadcasted_iota(jnp.int32, (per, LANES), 1)
        score = jnp.sum(total[:, width:], axis=1, keepdims=True)
        outs[i][:, pl.ds(width, LANES)] = split_score(score, lane)


def pair_sum(keep, got, n_out):
    rows, width = keep.shape
    outs = [jax.ShapeDtypeStruct((rows // n_out, width), BF16) for _ in range(n_out)]
    return call(
        functools.partial(pair_body, n_out),
        "pair_sum",
        outs,
        (keep, got),
        [vmem_spec()] * 2,
        [],
        4 * MIB + 6 * nbytes(keep.shape, BF16),
    )


def owner_body(n_in, *refs):
    ins = refs[:n_in]
    outs = refs[n_in:]
    width = ins[0].shape[1] - LANES
    total = ins[0][...].astype(F32)
    for ref in ins[1:]:
        total = total + ref[...].astype(F32)
    score = jnp.sum(total[:, width:], axis=1, keepdims=True)
    lane = lax.broadcasted_iota(jnp.int32, (ins[0].shape[0], LANES), 1)
    tail = jnp.where(lane == 0, score, 0.0)
    for k, out in enumerate(outs):
        span = slice(k * CAP, (k + 1) * CAP)
        out[:, :width] = total[span, :width].astype(BF16)
        out[:, pl.ds(width, LANES)] = tail[span].astype(BF16)


def owner_sum(parts, n_out):
    rows, width = parts[0].shape
    outs = [jax.ShapeDtypeStruct((rows // n_out, width), BF16) for _ in range(n_out)]
    return call(
        functools.partial(owner_body, len(parts)),
        "owner_sum",
        outs,
        tuple(parts),
        [vmem_spec()] * len(parts),
        [],
        4 * MIB + 8 * nbytes(parts[0].shape, F32),
    )


def final_body(n_exp, cols, *refs):
    msgs = refs[:n_exp]
    weight_ref, chosen_ref, ids_ref, dtok_ref, dgate_ref, lhs, tail = refs[n_exp:]
    width = msgs[0].shape[1] - LANES
    rows, top = ids_ref.shape
    slots = n_exp * CAP
    step = pl.program_id(0)

    @pl.when(step == 0)
    def _():
        weight = weight_ref[...]
        high = weight.astype(BF16).astype(F32)
        rest = weight - high
        mid = rest.astype(BF16).astype(F32)
        low = rest - mid
        packed = high + pltpu.roll(mid, slots, 1) + pltpu.roll(low, 2 * slots, 1)
        lhs[...] = packed.astype(BF16)
        tail[...] = jnp.zeros_like(tail)
        for k in range(n_exp):
            tail[k * CAP : (k + 1) * CAP, :] = msgs[k][:, pl.ds(width, LANES)].astype(F32)
        score = tail[...].T[:1]
        kept = chosen_ref[...] * score
        lane = lax.broadcasted_iota(jnp.int32, (rows, LANES), 1)
        expert = jnp.where(
            lane < slots, (lane >> (CAP.bit_length() - 1)) ^ lax.axis_index("exp"), -1
        )
        ids = ids_ref[...]
        spot = lax.broadcasted_iota(jnp.int32, (rows, top), 1)
        grads = jnp.zeros((rows, top), F32)
        for j in range(top):
            value = jnp.where(ids[:, j : j + 1] == expert, kept, 0.0)
            grads = jnp.where(spot == j, jnp.sum(value, axis=1, keepdims=True), grads)
        dgate_ref[...] = grads.astype(BF16)

    span = pl.ds(pl.multiple_of(step * cols, LANES), cols)
    stacked = jnp.concatenate([msg[:, span] for msg in msgs] * 3, axis=0)
    out = jnp.dot(lhs[:, : 3 * slots], stacked, preferred_element_type=F32)
    dtok_ref[...] = out.astype(BF16)


def final(msgs, weight, chosen, expert_ids):
    n_exp = len(msgs)
    width = msgs[0].shape[1] - LANES
    rows, top = expert_ids.shape
    cols = width // 4
    whole = lambda shape: pl.BlockSpec(shape, lambda i: (0, 0))
    return pl.pallas_call(
        functools.partial(final_body, n_exp, cols),
        grid=(width // cols,),
        in_specs=[whole(m.shape) for m in msgs]
        + [whole(weight.shape), whole(chosen.shape), whole(expert_ids.shape)],
        out_specs=[pl.BlockSpec((rows, cols), lambda i: (0, i)), whole((rows, top))],
        out_shape=[
            jax.ShapeDtypeStruct((rows, width), BF16),
            jax.ShapeDtypeStruct((rows, top), BF16),
        ],
        scratch_shapes=[pltpu.VMEM((rows, LANES), BF16), pltpu.VMEM((LANES, LANES), F32)],
        compiler_params=pltpu.CompilerParams(vmem_limit_bytes=12 * MIB),
        cost_estimate=pl.CostEstimate(
            flops=2 * rows * LANES * width, bytes_accessed=2 * rows * width, transcendentals=0
        ),
        name="final",
    )(*msgs, weight, chosen, expert_ids)


def gather_blocks(own, n_ctx):
    blocks = {0: own}
    for j in range(2, n_ctx, 2):
        blocks[j] = exchange(own, "ctx", j)
    for j in range(0, n_ctx, 2):
        blocks[j + 1] = exchange(blocks[j], "ctx", 1)
    return [blocks[j] for j in range(n_ctx)]


def widen_add(*arrays):
    total = arrays[0].astype(F32)
    for array in arrays[1:]:
        total = total + array.astype(F32)
    return total.astype(BF16)


def local(
    queries,
    latent,
    grad_out,
    doc_ids,
    tokens,
    token_grads,
    gate_values,
    expert_ids,
    gate_order,
    w_gate,
    w_up,
    w_down,
):
    n_ctx = lax.axis_size("ctx")
    n_exp = lax.axis_size("exp")
    assert w_gate.shape[0] == 1
    per_dev = latent.shape[0]

    sends, weight, chosen = route(
        expert_ids, gate_order, gate_values, tokens, token_grads, n_exp
    )
    got = [sends[0]] + [exchange(sends[k], "exp", k) for k in range(1, n_exp)]
    own_rows = jnp.concatenate([g[:CAP] for g in got] + [g[CAP:] for g in got], axis=0)

    doc_cols = jnp.broadcast_to(doc_ids.astype(BF16)[:, None], (per_dev, LANES))
    lat_blocks = gather_blocks(jnp.concatenate([latent, doc_cols], axis=1), n_ctx)
    row_blocks = gather_blocks(own_rows, n_ctx)

    d_queries, lat_even, lat_odd = attention(queries, grad_out, lat_blocks)
    lat_sum = widen_add(lat_even, exchange(lat_odd, "ctx", 1))
    lat_parts = [lat_sum[:per_dev]]
    for i in range(1, n_ctx // 2):
        lat_parts.append(exchange(lat_sum[i * per_dev : (i + 1) * per_dev], "ctx", 2 * i))
    lat_total = widen_add(*lat_parts)
    mask = 1
    while mask < n_exp:
        lat_total = widen_add(lat_total, exchange(lat_total, "exp", mask))
        mask *= 2

    even, odd = experts(row_blocks, w_gate, w_up, w_down)
    summed = pair_sum(even, exchange(odd, "ctx", 1), n_ctx // 2)
    parts = [summed[0]] + [exchange(summed[i], "ctx", 2 * i) for i in range(1, n_ctx // 2)]
    backs = owner_sum(parts, n_exp)
    back = [backs[0]] + [exchange(backs[k], "exp", k) for k in range(1, n_exp)]
    d_tokens, d_gates = final(back, weight, chosen, expert_ids)
    return (d_queries, lat_total, d_tokens, d_gates)


def solution(mesh):
    in_specs = (
        P("ctx", "exp", None),
        P("ctx", None),
        P("ctx", "exp", None),
        P("ctx"),
        P(("ctx", "exp"), None),
        P(("ctx", "exp"), None),
        P(("ctx", "exp"), None),
        P(("ctx", "exp"), None),
        P(("ctx", "exp"), None),
        P("exp", None, "ctx"),
        P("exp", None, "ctx"),
        P("exp", "ctx", None),
    )
    out_specs = (
        P("ctx", "exp", None),
        P("ctx", None),
        P(("ctx", "exp"), None),
        P(("ctx", "exp"), None),
    )
    return jax.shard_map(local, mesh=mesh, in_specs=in_specs, out_specs=out_specs, check_vma=False)
```

```python
import functools

import jax
import jax.numpy as jnp
from jax import lax
from jax.experimental import pallas as pl
from jax.experimental.pallas import tpu as pltpu
from jax.sharding import PartitionSpec as P


SCALE_DIM = 192
CAP = 2
LANES = 128
MIB = 1 << 20
F32 = jnp.float32
BF16 = jnp.bfloat16


def exchange(array, axis, mask):
    count = lax.axis_size(axis)
    return lax.ppermute(array, axis, [(i, i ^ mask) for i in range(count)])


def turned(place):
    return (place & ~3) | ((place & 1) << 1) | ((place & 2) >> 1)


def chip_exchange(array, place):
    count = lax.axis_size("ctx")
    pairs = [(i, i ^ (2 * (turned(place) if i & 1 else place))) for i in range(count)]
    return lax.ppermute(array, "ctx", pairs)


def core_exchange(array):
    return exchange(array, "ctx", 1)


def vmem_spec():
    return pl.BlockSpec(memory_space=pltpu.VMEM)


def hbm_spec():
    return pl.BlockSpec(memory_space=pltpu.HBM)


def nbytes(shape, dtype):
    total = jnp.dtype(dtype).itemsize
    for size in shape:
        total *= size
    return total


def call(body, outs, args, in_specs, scratch, limit, flops=0, out_specs=None):
    moved = sum(nbytes(a.shape, a.dtype) for a in args)
    moved += sum(nbytes(o.shape, o.dtype) for o in outs)
    args = [
        pltpu.with_memory_space_constraint(a, pltpu.HBM) if s.memory_space == pltpu.HBM else a
        for a, s in zip(args, in_specs)
    ]
    return pl.pallas_call(
        body,
        out_shape=outs,
        in_specs=in_specs,
        out_specs=out_specs or [vmem_spec() for _ in outs],
        scratch_shapes=scratch,
        compiler_params=pltpu.CompilerParams(vmem_limit_bytes=limit),
        cost_estimate=pl.CostEstimate(flops=flops, bytes_accessed=moved, transcendentals=0),
    )(*args)


def slot_experts(shape):
    slot = lax.broadcasted_iota(jnp.int32, shape, 0)
    return (slot >> (CAP.bit_length() - 1)) ^ lax.axis_index("exp")


def route_body(n_exp, ids_hbm, order_hbm, gates_hbm, tok_hbm, grad_hbm, *rest):
    msgs = rest[:n_exp]
    weight_ref, chosen_ref, ids_ref, order_ref, gates_ref, held, sems = rest[n_exp:]
    pieces = 2
    width = held.shape[2]
    piece = width // pieces
    small = [
        pltpu.make_async_copy(src, dst, sems.at[i])
        for i, (src, dst) in enumerate(
            ((ids_hbm, ids_ref), (order_hbm, order_ref), (gates_hbm, gates_ref))
        )
    ]
    large = [
        pltpu.make_async_copy(
            src.at[:, pl.ds(c * piece, piece)],
            held.at[i, :, pl.ds(c * piece, piece)],
            sems.at[3 + i * pieces + c],
        )
        for c in range(pieces)
        for i, src in enumerate((tok_hbm, grad_hbm))
    ]
    for copy in small + large:
        copy.start()
    for copy in small:
        copy.wait()
    top, rows = ids_ref.shape
    shape = (n_exp * CAP, rows)
    expert = slot_experts(shape)
    ids = ids_ref[...]
    gates = gates_ref[...]
    hits = jnp.zeros(shape, F32)
    mass = jnp.zeros(shape, F32)
    for j in range(top):
        match = ids[j : j + 1] == expert
        hits = hits + jnp.where(match, 1.0, 0.0)
        mass = mass + jnp.where(match, gates[j : j + 1], 0.0)
    order = jnp.broadcast_to(order_ref[...].astype(F32), (rows, rows))
    earlier = jnp.where(order.T < order, 1.0, 0.0).astype(BF16)
    ranks = jnp.dot(hits.astype(BF16), earlier, preferred_element_type=F32)
    slot = (lax.broadcasted_iota(jnp.int32, shape, 0) & (CAP - 1)).astype(F32)
    chosen = jnp.where((hits == 1.0) & (ranks == slot), 1.0, 0.0)
    weight_ref[...] = chosen * mass
    chosen_ref[...] = chosen
    pick = chosen.astype(BF16)
    for c in range(pieces):
        large[2 * c].wait()
        large[2 * c + 1].wait()
        cols = pl.ds(c * piece, piece)
        tok = jnp.dot(pick, held[0, :, cols], preferred_element_type=F32)
        grad = jnp.dot(pick, held[1, :, cols], preferred_element_type=F32)
        for k in range(n_exp):
            span = slice(k * CAP, (k + 1) * CAP)
            msgs[k][:, cols] = jnp.concatenate([tok[span], grad[span]], axis=0).astype(BF16)


def route(expert_ids, gate_order, gate_values, tokens, token_grads, n_exp):
    rows, width = tokens.shape
    top = expert_ids.shape[1]
    outs = [jax.ShapeDtypeStruct((2 * CAP, width), BF16) for _ in range(n_exp)]
    outs += [jax.ShapeDtypeStruct((n_exp * CAP, rows), F32)] * 2
    res = call(
        functools.partial(route_body, n_exp),
        outs,
        (expert_ids.T, gate_order, gate_values.T, tokens, token_grads),
        [hbm_spec()] * 5,
        [
            pltpu.VMEM((top, rows), jnp.int32),
            pltpu.VMEM((1, rows), jnp.int32),
            pltpu.VMEM((top, rows), F32),
            pltpu.VMEM((2, rows, width), BF16),
            pltpu.SemaphoreType.DMA((7,)),
        ],
        12 * MIB,
        flops=4 * n_exp * CAP * rows * width,
    )
    return res[:n_exp], res[n_exp], res[n_exp + 1]


def attention_body(n_ctx, heads, row_block, *refs):
    q_ref, go_ref = refs[:2]
    blocks = refs[2 : 2 + n_ctx]
    w_hbm = refs[2 + n_ctx : 5 + n_ctx]
    dq_hbm, even_ref, odd_ref = refs[5 + n_ctx : 8 + n_ctx]
    w_vmem = refs[8 + n_ctx : 11 + n_ctx]
    lat, dq, dq_sems, w_sems = refs[11 + n_ctx :]
    fetches = [
        pltpu.make_async_copy(src.at[0], dst, w_sems.at[i])
        for i, (src, dst) in enumerate(zip(w_hbm, w_vmem))
    ]
    for fetch in fetches:
        fetch.start()
    per = blocks[0].shape[0]
    rows, width = q_ref.shape
    scale = SCALE_DIM ** (-0.5)
    keydoc = []
    for i, block in enumerate(blocks):
        lat[i * per : (i + 1) * per, :] = block[:, :width]
        keydoc.append(block[:, width:].astype(F32))
    keydoc = jnp.concatenate(keydoc, axis=0)
    reps = row_block // LANES
    if reps > 1:
        keydoc = jnp.concatenate([keydoc] * reps, axis=1)
    keys = lat[...]
    nt = (((1,), (1,)), ((), ()))
    tn = (((0,), (0,)), ((), ()))
    owner = lax.broadcasted_iota(jnp.int32, (per, row_block), 0)
    col = lax.broadcasted_iota(jnp.int32, (per, row_block), 1)
    acc = None
    writes = []
    for b in range(rows // row_block):
        span = pl.ds(b * row_block, row_block)
        q = q_ref[span, :]
        go = go_ref[span, :]
        at = col + b * row_block
        spread = jnp.where((at >= owner * heads) & (at < (owner + 1) * heads), 1.0, 0.0)
        qdoc = lax.dot_general(
            blocks[0][:, width:], spread.astype(BF16), tn, preferred_element_type=F32
        )[:1]
        scores = lax.dot_general(keys, q, nt, preferred_element_type=F32) * scale
        scores = jnp.where(keydoc == qdoc, scores, -1e30)
        top = jnp.max(scores, axis=0, keepdims=True)
        probs = jnp.exp(scores - top)
        total = jnp.sum(probs, axis=0, keepdims=True)
        probs = probs * (1.0 / total)
        pgrad = lax.dot_general(keys, go, nt, preferred_element_type=F32)
        delta = jnp.sum(probs * pgrad, axis=0, keepdims=True)
        sgrad = (probs * (pgrad - delta)).astype(BF16)
        probs = probs.astype(BF16)
        dq[span, :] = (
            lax.dot_general(sgrad, keys, tn, preferred_element_type=F32) * scale
        ).astype(BF16)
        write = pltpu.make_async_copy(dq.at[span, :], dq_hbm.at[span, :], dq_sems.at[b])
        write.start()
        writes.append(write)
        term = jnp.dot(sgrad, q, preferred_element_type=F32) * scale
        term = term + jnp.dot(probs, go, preferred_element_type=F32)
        acc = term if acc is None else acc + term
    half = even_ref.shape[0]
    even_ref[...] = acc[:half, :].astype(BF16)
    odd_ref[...] = acc[half:, :].astype(BF16)
    for copy in writes + fetches:
        copy.wait()


def attention(queries, grad_out, blocks, weights):
    n_ctx = len(blocks)
    q_rows, heads, width = queries.shape
    rows = q_rows * heads
    keys = blocks[0].shape[0] * n_ctx
    row_block = min(256, rows)
    q = queries.reshape(rows, width)
    go = grad_out.reshape(rows, width)
    half = (keys // 2, width)
    outs = [
        jax.ShapeDtypeStruct((rows, width), BF16),
        jax.ShapeDtypeStruct(half, BF16),
        jax.ShapeDtypeStruct(half, BF16),
    ]
    outs += [pltpu.VMEM(w.shape[1:], BF16) for w in weights]
    res = call(
        functools.partial(attention_body, n_ctx, heads, row_block),
        outs,
        (q, go, *blocks, *weights),
        [vmem_spec()] * (2 + n_ctx) + [hbm_spec()] * 3,
        [
            pltpu.VMEM((keys, width), BF16),
            pltpu.VMEM((rows, width), BF16),
            pltpu.SemaphoreType.DMA((rows // row_block,)),
            pltpu.SemaphoreType.DMA((3,)),
        ],
        24 * MIB,
        flops=10 * rows * keys * width,
        out_specs=[hbm_spec()] + [vmem_spec()] * 5,
    )
    return res[0].reshape(queries.shape), res[1], res[2], res[3:]


def split_score(total, lane):
    high = total.astype(BF16).astype(F32)
    low = total - high
    return jnp.where(lane == 0, high, jnp.where(lane == 1, low, 0.0)).astype(BF16)


def expert_body(n_ctx, chunks, *refs):
    blocks = refs[:n_ctx]
    wg, wu, wd, even_ref, odd_ref, xt, xg = refs[n_ctx:]
    width, hid = wg.shape
    step = width // chunks
    per = blocks[0].shape[0] // 2
    for i, block in enumerate(blocks):
        xt[i * per : (i + 1) * per, :] = block[:per, :]
        xg[i * per : (i + 1) * per, :] = block[per:, :]
    rows = per * n_ctx
    nt = (((1,), (1,)), ((), ()))
    gate = jnp.zeros((rows, hid), F32)
    up = jnp.zeros((rows, hid), F32)
    act = jnp.zeros((rows, hid), F32)
    for c in range(chunks):
        cols = pl.ds(c * step, step)
        gate = gate + jnp.dot(xt[:, cols], wg[cols, :], preferred_element_type=F32)
        up = up + jnp.dot(xt[:, cols], wu[cols, :], preferred_element_type=F32)
        act = act + lax.dot_general(xg[:, cols], wd[:, cols], nt, preferred_element_type=F32)
    sig = jax.nn.sigmoid(gate)
    silu = gate * sig
    hidden = (silu * up).astype(BF16).astype(F32)
    score = jnp.sum(hidden * act, axis=1, keepdims=True)
    ggrad = (act * up * sig * (1.0 + gate * (1.0 - sig))).astype(BF16)
    ugrad = (act * silu).astype(BF16)
    half = rows // 2
    lane = lax.broadcasted_iota(jnp.int32, (rows, LANES), 1)
    tail = split_score(score, lane)
    even_ref[:, pl.ds(width, LANES)] = tail[:half]
    odd_ref[:, pl.ds(width, LANES)] = tail[half:]
    fine = 512
    for c in range(width // fine):
        cols = pl.ds(c * fine, fine)
        part = lax.dot_general(ggrad, wg[cols, :], nt, preferred_element_type=F32)
        part = part + lax.dot_general(ugrad, wu[cols, :], nt, preferred_element_type=F32)
        part = part.astype(BF16)
        even_ref[:, cols] = part[:half]
        odd_ref[:, cols] = part[half:]


def experts(blocks, weights):
    n_ctx = len(blocks)
    width = blocks[0].shape[1]
    hid = weights[0].shape[1]
    rows = blocks[0].shape[0] // 2 * n_ctx
    out = jax.ShapeDtypeStruct((rows // 2, width + LANES), BF16)
    weights = [pltpu.with_memory_space_constraint(w, pltpu.VMEM) for w in weights]
    return call(
        functools.partial(expert_body, n_ctx, 4),
        [out, out],
        (*blocks, *weights),
        [vmem_spec()] * (n_ctx + 3),
        [pltpu.VMEM((rows, width), BF16), pltpu.VMEM((rows, width), BF16)],
        min(30 * MIB, 4 * MIB + 6 * nbytes((rows, width), BF16)),
        flops=10 * rows * width * hid,
    )


def pair_body(n_out, keep_ref, got_ref, *outs):
    width = outs[0].shape[1] - LANES
    per = outs[0].shape[0]
    for i in range(n_out):
        span = pl.ds(i * per, per)
        total = keep_ref[span, :].astype(F32) + got_ref[span, :].astype(F32)
        outs[i][:, :width] = total[:, :width].astype(BF16)
        lane = lax.broadcasted_iota(jnp.int32, (per, LANES), 1)
        score = jnp.sum(total[:, width:], axis=1, keepdims=True)
        outs[i][:, pl.ds(width, LANES)] = split_score(score, lane)


def pair_sum(keep, got, n_out):
    rows, width = keep.shape
    outs = [jax.ShapeDtypeStruct((rows // n_out, width), BF16) for _ in range(n_out)]
    return call(
        functools.partial(pair_body, n_out),
        outs,
        (keep, got),
        [vmem_spec()] * 2,
        [],
        4 * MIB + 6 * nbytes(keep.shape, BF16),
    )


def owner_body(n_in, *refs):
    ins = refs[:n_in]
    outs = refs[n_in:]
    width = ins[0].shape[1] - LANES
    total = ins[0][...].astype(F32)
    for ref in ins[1:]:
        total = total + ref[...].astype(F32)
    score = jnp.sum(total[:, width:], axis=1, keepdims=True)
    lane = lax.broadcasted_iota(jnp.int32, (ins[0].shape[0], LANES), 1)
    tail = jnp.where(lane == 0, score, 0.0)
    for k, out in enumerate(outs):
        span = slice(k * CAP, (k + 1) * CAP)
        out[:, :width] = total[span, :width].astype(BF16)
        out[:, pl.ds(width, LANES)] = tail[span].astype(BF16)


def owner_sum(parts, n_out):
    rows, width = parts[0].shape
    outs = [jax.ShapeDtypeStruct((rows // n_out, width), BF16) for _ in range(n_out)]
    return call(
        functools.partial(owner_body, len(parts)),
        outs,
        tuple(parts),
        [vmem_spec()] * len(parts),
        [],
        4 * MIB + 8 * nbytes(parts[0].shape, F32),
    )


def final_body(n_exp, chunks, *refs):
    msgs = refs[:n_exp]
    weight_ref, chosen_ref, ids_ref, dtok_hbm, dgate_ref, out, sems = refs[n_exp:]
    width = msgs[0].shape[1] - LANES
    top, rows = ids_ref.shape
    slots = n_exp * CAP
    weight = weight_ref[...]
    high = weight.astype(BF16)
    rest = weight - high.astype(F32)
    mid = rest.astype(BF16)
    low = (rest - mid.astype(F32)).astype(BF16)
    lhs = jnp.concatenate([high, mid, low], axis=0)
    tn = (((0,), (0,)), ((), ()))
    step = width // chunks
    writes = []
    for c in range(chunks):
        cols = pl.ds(c * step, step)
        piece = jnp.concatenate([msg[:, cols] for msg in msgs], axis=0)
        stacked = jnp.concatenate([piece] * 3, axis=0)
        out[:, cols] = lax.dot_general(lhs, stacked, tn, preferred_element_type=F32).astype(BF16)
        write = pltpu.make_async_copy(out.at[:, cols], dtok_hbm.at[:, cols], sems.at[c])
        write.start()
        writes.append(write)
    tail = jnp.concatenate([msg[:, pl.ds(width, LANES)] for msg in msgs], axis=0)
    kept = chosen_ref[...] * tail[:, :1].astype(F32)
    expert = slot_experts((slots, rows))
    ids = ids_ref[...]
    grads = [
        jnp.sum(jnp.where(ids[j : j + 1] == expert, kept, 0.0), axis=0, keepdims=True)
        for j in range(top)
    ]
    dgate_ref[...] = jnp.concatenate(grads, axis=0).astype(BF16)
    for write in writes:
        write.wait()


def final(msgs, weight, chosen, expert_ids):
    n_exp = len(msgs)
    width = msgs[0].shape[1] - LANES
    rows, top = expert_ids.shape
    chunks = 4
    d_tokens, d_gates = call(
        functools.partial(final_body, n_exp, chunks),
        [
            jax.ShapeDtypeStruct((rows, width), BF16),
            jax.ShapeDtypeStruct((top, rows), BF16),
        ],
        (*msgs, weight, chosen, expert_ids.T),
        [vmem_spec()] * (n_exp + 3),
        [pltpu.VMEM((rows, width), BF16), pltpu.SemaphoreType.DMA((chunks,))],
        12 * MIB,
        flops=6 * n_exp * CAP * rows * width,
        out_specs=[hbm_spec(), vmem_spec()],
    )
    return d_tokens, d_gates.T


def gather_blocks(own, n_ctx):
    chips = n_ctx // 2
    line = [own] + [chip_exchange(own, p) for p in range(1, chips)]
    return line + [core_exchange(block) for block in line]


def widen_add(*arrays):
    total = arrays[0].astype(F32)
    for array in arrays[1:]:
        total = total + array.astype(F32)
    return total.astype(BF16)


def local(
    queries,
    latent,
    grad_out,
    doc_ids,
    tokens,
    token_grads,
    gate_values,
    expert_ids,
    gate_order,
    w_gate,
    w_up,
    w_down,
):
    n_ctx = lax.axis_size("ctx")
    n_exp = lax.axis_size("exp")
    assert w_gate.shape[0] == 1
    per_dev = latent.shape[0]

    chips = n_ctx // 2
    sends, weight, chosen = route(
        expert_ids, gate_order, gate_values, tokens, token_grads, n_exp
    )
    got = [sends[0]] + [exchange(sends[k], "exp", k) for k in range(1, n_exp)]
    own_rows = jnp.concatenate([g[:CAP] for g in got] + [g[CAP:] for g in got], axis=0)

    doc_cols = jnp.broadcast_to(doc_ids.astype(BF16)[:, None], (per_dev, LANES))
    lat_blocks = gather_blocks(jnp.concatenate([latent, doc_cols], axis=1), n_ctx)
    row_blocks = gather_blocks(own_rows, n_ctx)

    d_queries, lat_even, lat_odd, weights = attention(
        queries, grad_out, lat_blocks, (w_gate, w_up, w_down)
    )
    lat_sum = widen_add(lat_even, core_exchange(lat_odd))
    lat_parts = [lat_sum[:per_dev]]
    for p in range(1, chips):
        part = lat_sum[p * per_dev : (p + 1) * per_dev]
        lat_parts.append(chip_exchange(part, p))
    lat_total = widen_add(*lat_parts)
    mask = 1
    while mask < n_exp:
        lat_total = widen_add(lat_total, exchange(lat_total, "exp", mask))
        mask *= 2

    even, odd = experts(row_blocks, weights)
    summed = pair_sum(even, core_exchange(odd), chips)
    parts = [summed[0]] + [chip_exchange(summed[p], p) for p in range(1, chips)]
    backs = owner_sum(parts, n_exp)
    back = [backs[0]] + [exchange(backs[k], "exp", k) for k in range(1, n_exp)]
    d_tokens, d_gates = final(back, weight, chosen, expert_ids)
    return (d_queries, lat_total, d_tokens, d_gates)


def solution(mesh):
    in_specs = (
        P("ctx", "exp", None),
        P("ctx", None),
        P("ctx", "exp", None),
        P("ctx"),
        P(("ctx", "exp"), None),
        P(("ctx", "exp"), None),
        P(("ctx", "exp"), None),
        P(("ctx", "exp"), None),
        P(("ctx", "exp"), None),
        P("exp", None, "ctx"),
        P("exp", None, "ctx"),
        P("exp", "ctx", None),
    )
    out_specs = (
        P("ctx", "exp", None),
        P("ctx", None),
        P(("ctx", "exp"), None),
        P(("ctx", "exp"), None),
    )
    return jax.shard_map(local, mesh=mesh, in_specs=in_specs, out_specs=out_specs, check_vma=False)
```

```python
import functools

import jax
import jax.numpy as jnp
from jax import lax
from jax.experimental import pallas as pl
from jax.experimental.pallas import tpu as pltpu
from jax.sharding import PartitionSpec as P


SCALE_DIM = 192
CAP = 2
LANES = 128
MIB = 1 << 20
F32 = jnp.float32
BF16 = jnp.bfloat16


def exchange(array, axis, mask):
    count = lax.axis_size(axis)
    return lax.ppermute(array, axis, [(i, i ^ mask) for i in range(count)])


def turned(place):
    return (place & ~3) | ((place & 1) << 1) | ((place & 2) >> 1)


def chip_exchange(array, place):
    count = lax.axis_size("ctx")
    pairs = [(i, i ^ (2 * (turned(place) if i & 1 else place))) for i in range(count)]
    return lax.ppermute(array, "ctx", pairs)


def core_exchange(array):
    return exchange(array, "ctx", 1)


def vmem_spec():
    return pl.BlockSpec(memory_space=pltpu.VMEM)


def hbm_spec():
    return pl.BlockSpec(memory_space=pltpu.HBM)


def nbytes(shape, dtype):
    total = jnp.dtype(dtype).itemsize
    for size in shape:
        total *= size
    return total


def call(body, outs, args, in_specs, scratch, limit, flops=0, out_specs=None):
    moved = sum(nbytes(a.shape, a.dtype) for a in args)
    moved += sum(nbytes(o.shape, o.dtype) for o in outs)
    args = [
        pltpu.with_memory_space_constraint(a, pltpu.HBM) if s.memory_space == pltpu.HBM else a
        for a, s in zip(args, in_specs)
    ]
    return pl.pallas_call(
        body,
        out_shape=outs,
        in_specs=in_specs,
        out_specs=out_specs or [vmem_spec() for _ in outs],
        scratch_shapes=scratch,
        compiler_params=pltpu.CompilerParams(vmem_limit_bytes=limit),
        cost_estimate=pl.CostEstimate(flops=flops, bytes_accessed=moved, transcendentals=0),
    )(*args)


def halvings(count):
    return [count >> i for i in range(1, count.bit_length())]


def slot_experts(shape):
    slot = lax.broadcasted_iota(jnp.int32, shape, 0)
    return (slot >> (CAP.bit_length() - 1)) ^ lax.axis_index("exp")


def route_body(n_exp, ids_hbm, order_hbm, gates_hbm, tok_hbm, grad_hbm, *rest):
    msgs = rest[:n_exp]
    weight_ref, chosen_ref, ids_ref, order_ref, gates_ref, held, sems = rest[n_exp:]
    pieces = 4
    width = held.shape[2]
    piece = width // pieces
    small = [
        pltpu.make_async_copy(src, dst, sems.at[i])
        for i, (src, dst) in enumerate(
            ((ids_hbm, ids_ref), (order_hbm, order_ref), (gates_hbm, gates_ref))
        )
    ]
    large = [
        pltpu.make_async_copy(
            src.at[:, pl.ds(c * piece, piece)],
            held.at[i, :, pl.ds(c * piece, piece)],
            sems.at[3 + i * pieces + c],
        )
        for c in range(pieces)
        for i, src in enumerate((tok_hbm, grad_hbm))
    ]
    for copy in small + large:
        copy.start()
    for copy in small:
        copy.wait()
    top, rows = ids_ref.shape
    shape = (n_exp * CAP, rows)
    expert = slot_experts(shape)
    ids = ids_ref[...]
    gates = gates_ref[...]
    hits = jnp.zeros(shape, F32)
    mass = jnp.zeros(shape, F32)
    for j in range(top):
        match = ids[j : j + 1] == expert
        hits = hits + jnp.where(match, 1.0, 0.0)
        mass = mass + jnp.where(match, gates[j : j + 1], 0.0)
    order = jnp.broadcast_to(order_ref[...].astype(F32), (rows, rows))
    earlier = jnp.where(order.T < order, 1.0, 0.0).astype(BF16)
    ranks = jnp.dot(hits.astype(BF16), earlier, preferred_element_type=F32)
    slot = (lax.broadcasted_iota(jnp.int32, shape, 0) & (CAP - 1)).astype(F32)
    chosen = jnp.where((hits == 1.0) & (ranks == slot), 1.0, 0.0)
    weight_ref[...] = chosen * mass
    chosen_ref[...] = chosen
    pick = chosen.astype(BF16)
    for c in range(pieces):
        large[2 * c].wait()
        large[2 * c + 1].wait()
        cols = pl.ds(c * piece, piece)
        tok = jnp.dot(pick, held[0, :, cols], preferred_element_type=F32)
        grad = jnp.dot(pick, held[1, :, cols], preferred_element_type=F32)
        for k in range(n_exp):
            span = slice(k * CAP, (k + 1) * CAP)
            msgs[k][:, cols] = jnp.concatenate([tok[span], grad[span]], axis=0).astype(BF16)


def route(expert_ids, gate_order, gate_values, tokens, token_grads, n_exp):
    rows, width = tokens.shape
    top = expert_ids.shape[1]
    outs = [jax.ShapeDtypeStruct((2 * CAP, width), BF16) for _ in range(n_exp)]
    outs += [jax.ShapeDtypeStruct((n_exp * CAP, rows), F32)] * 2
    res = call(
        functools.partial(route_body, n_exp),
        outs,
        (expert_ids.T, gate_order, gate_values.T, tokens, token_grads),
        [hbm_spec()] * 5,
        [
            pltpu.VMEM((top, rows), jnp.int32),
            pltpu.VMEM((1, rows), jnp.int32),
            pltpu.VMEM((top, rows), F32),
            pltpu.VMEM((2, rows, width), BF16),
            pltpu.SemaphoreType.DMA((11,)),
        ],
        12 * MIB,
        flops=4 * n_exp * CAP * rows * width,
    )
    return res[:n_exp], res[n_exp], res[n_exp + 1]


def attention_body(n_blocks, heads, row_block, *refs):
    q_ref, go_ref = refs[:2]
    blocks = refs[2 : 2 + n_blocks]
    w_hbm = refs[2 + n_blocks : 5 + n_blocks]
    dq_hbm, even_ref, odd_ref = refs[5 + n_blocks : 8 + n_blocks]
    w_vmem = refs[8 + n_blocks : 11 + n_blocks]
    lat, dq, dq_sems, w_sems = refs[11 + n_blocks :]
    fetches = [
        pltpu.make_async_copy(src.at[0], dst, w_sems.at[i])
        for i, (src, dst) in enumerate(zip(w_hbm, w_vmem))
    ]
    for fetch in fetches:
        fetch.start()
    rows, width = q_ref.shape
    per = rows // heads
    scale = SCALE_DIM ** (-0.5)
    keydoc = []
    at = 0
    for block in blocks:
        lat[at : at + block.shape[0], :] = block[:, :width]
        keydoc.append(block[:, width:].astype(F32))
        at += block.shape[0]
    keydoc = jnp.concatenate(keydoc, axis=0)
    reps = row_block // LANES
    if reps > 1:
        keydoc = jnp.concatenate([keydoc] * reps, axis=1)
    keys = lat[...]
    nt = (((1,), (1,)), ((), ()))
    tn = (((0,), (0,)), ((), ()))
    owner = lax.broadcasted_iota(jnp.int32, (per, row_block), 0)
    col = lax.broadcasted_iota(jnp.int32, (per, row_block), 1)
    acc = None
    writes = []
    for b in range(rows // row_block):
        span = pl.ds(b * row_block, row_block)
        q = q_ref[span, :]
        go = go_ref[span, :]
        at = col + b * row_block
        spread = jnp.where((at >= owner * heads) & (at < (owner + 1) * heads), 1.0, 0.0)
        qdoc = lax.dot_general(
            blocks[0][:per, width:], spread.astype(BF16), tn, preferred_element_type=F32
        )[:1]
        scores = lax.dot_general(keys, q, nt, preferred_element_type=F32) * scale
        scores = jnp.where(keydoc == qdoc, scores, -1e30)
        top = jnp.max(scores, axis=0, keepdims=True)
        probs = jnp.exp(scores - top)
        total = jnp.sum(probs, axis=0, keepdims=True)
        probs = probs * (1.0 / total)
        pgrad = lax.dot_general(keys, go, nt, preferred_element_type=F32)
        delta = jnp.sum(probs * pgrad, axis=0, keepdims=True)
        sgrad = (probs * (pgrad - delta)).astype(BF16)
        probs = probs.astype(BF16)
        dq[span, :] = (
            lax.dot_general(sgrad, keys, tn, preferred_element_type=F32) * scale
        ).astype(BF16)
        write = pltpu.make_async_copy(dq.at[span, :], dq_hbm.at[span, :], dq_sems.at[b])
        write.start()
        writes.append(write)
        term = jnp.dot(sgrad, q, preferred_element_type=F32) * scale
        term = term + jnp.dot(probs, go, preferred_element_type=F32)
        acc = term if acc is None else acc + term
    half = even_ref.shape[0]
    even_ref[...] = acc[:half, :].astype(BF16)
    odd_ref[...] = acc[half:, :].astype(BF16)
    for copy in writes + fetches:
        copy.wait()


def attention(queries, grad_out, blocks, weights):
    n_blocks = len(blocks)
    q_rows, heads, width = queries.shape
    rows = q_rows * heads
    keys = sum(block.shape[0] for block in blocks)
    row_block = min(1024, rows)
    q = queries.reshape(rows, width)
    go = grad_out.reshape(rows, width)
    half = (keys // 2, width)
    outs = [
        jax.ShapeDtypeStruct((rows, width), BF16),
        jax.ShapeDtypeStruct(half, BF16),
        jax.ShapeDtypeStruct(half, BF16),
    ]
    outs += [pltpu.VMEM(w.shape[1:], BF16) for w in weights]
    res = call(
        functools.partial(attention_body, n_blocks, heads, row_block),
        outs,
        (q, go, *blocks, *weights),
        [vmem_spec()] * (2 + n_blocks) + [hbm_spec()] * 3,
        [
            pltpu.VMEM((keys, width), BF16),
            pltpu.VMEM((rows, width), BF16),
            pltpu.SemaphoreType.DMA((rows // row_block,)),
            pltpu.SemaphoreType.DMA((3,)),
        ],
        24 * MIB,
        flops=10 * rows * keys * width,
        out_specs=[hbm_spec()] + [vmem_spec()] * 5,
    )
    return res[0].reshape(queries.shape), res[1], res[2], res[3:]


def split_score(total, lane):
    high = total.astype(BF16).astype(F32)
    low = total - high
    return jnp.where(lane == 0, high, jnp.where(lane == 1, low, 0.0)).astype(BF16)


def expert_body(n_ctx, chunks, *refs):
    blocks = refs[:n_ctx]
    wg, wu, wd, even_ref, odd_ref, xt, xg = refs[n_ctx:]
    hid, width = wd.shape
    step = width // chunks
    per = blocks[0].shape[0] // 2
    for i, block in enumerate(blocks):
        xt[i * per : (i + 1) * per, :] = block[:per, :]
        xg[i * per : (i + 1) * per, :] = block[per:, :]
    rows = per * n_ctx
    nt = (((1,), (1,)), ((), ()))
    gate = jnp.zeros((rows, hid), F32)
    up = jnp.zeros((rows, hid), F32)
    act = jnp.zeros((rows, hid), F32)
    for c in range(chunks):
        cols = pl.ds(c * step, step)
        gate = gate + jnp.dot(xt[:, cols], wg[cols, :], preferred_element_type=F32)
        up = up + jnp.dot(xt[:, cols], wu[cols, :], preferred_element_type=F32)
        act = act + lax.dot_general(xg[:, cols], wd[:, cols], nt, preferred_element_type=F32)
    sig = jax.nn.sigmoid(gate)
    silu = gate * sig
    hidden = (silu * up).astype(BF16).astype(F32)
    score = jnp.sum(hidden * act, axis=1, keepdims=True)
    ggrad = (act * up * sig * (1.0 + gate * (1.0 - sig))).astype(BF16)
    ugrad = (act * silu).astype(BF16)
    half = rows // 2
    lane = lax.broadcasted_iota(jnp.int32, (rows, LANES), 1)
    tail = split_score(score, lane)
    even_ref[:, pl.ds(width, LANES)] = tail[:half]
    odd_ref[:, pl.ds(width, LANES)] = tail[half:]
    fine = 1024
    for c in range(width // fine):
        cols = pl.ds(c * fine, fine)
        part = lax.dot_general(ggrad, wg[cols, :], nt, preferred_element_type=F32)
        part = part + lax.dot_general(ugrad, wu[cols, :], nt, preferred_element_type=F32)
        part = part.astype(BF16)
        even_ref[:, cols] = part[:half]
        odd_ref[:, cols] = part[half:]


def experts(blocks, weights):
    n_ctx = len(blocks)
    width = blocks[0].shape[1]
    hid = weights[0].shape[1]
    rows = blocks[0].shape[0] // 2 * n_ctx
    out = jax.ShapeDtypeStruct((rows // 2, width + LANES), BF16)
    weights = [pltpu.with_memory_space_constraint(w, pltpu.VMEM) for w in weights]
    return call(
        functools.partial(expert_body, n_ctx, 7),
        [out, out],
        (*blocks, *weights),
        [vmem_spec()] * (n_ctx + 3),
        [pltpu.VMEM((rows, width), BF16), pltpu.VMEM((rows, width), BF16)],
        min(30 * MIB, 4 * MIB + 6 * nbytes((rows, width), BF16)),
        flops=10 * rows * width * hid,
    )


def pair_body(n_out, keep_ref, got_ref, *outs):
    width = outs[0].shape[1] - LANES
    per = outs[0].shape[0]
    for i in range(n_out):
        span = pl.ds(i * per, per)
        total = keep_ref[span, :].astype(F32) + got_ref[span, :].astype(F32)
        outs[i][:, :width] = total[:, :width].astype(BF16)
        lane = lax.broadcasted_iota(jnp.int32, (per, LANES), 1)
        score = jnp.sum(total[:, width:], axis=1, keepdims=True)
        outs[i][:, pl.ds(width, LANES)] = split_score(score, lane)


def pair_sum(keep, got, n_out):
    rows, width = keep.shape
    outs = [jax.ShapeDtypeStruct((rows // n_out, width), BF16) for _ in range(n_out)]
    return call(
        functools.partial(pair_body, n_out),
        outs,
        (keep, got),
        [vmem_spec()] * 2,
        [],
        4 * MIB + 6 * nbytes(keep.shape, BF16),
    )


def owner_body(n_in, *refs):
    ins = refs[:n_in]
    outs = refs[n_in:]
    width = ins[0].shape[1] - LANES
    total = ins[0][...].astype(F32)
    for ref in ins[1:]:
        total = total + ref[...].astype(F32)
    score = jnp.sum(total[:, width:], axis=1, keepdims=True)
    lane = lax.broadcasted_iota(jnp.int32, (ins[0].shape[0], LANES), 1)
    tail = jnp.where(lane == 0, score, 0.0)
    for k, out in enumerate(outs):
        span = slice(k * CAP, (k + 1) * CAP)
        out[:, :width] = total[span, :width].astype(BF16)
        out[:, pl.ds(width, LANES)] = tail[span].astype(BF16)


def owner_sum(parts, n_out):
    rows, width = parts[0].shape
    outs = [jax.ShapeDtypeStruct((rows // n_out, width), BF16) for _ in range(n_out)]
    return call(
        functools.partial(owner_body, len(parts)),
        outs,
        tuple(parts),
        [vmem_spec()] * len(parts),
        [],
        4 * MIB + 8 * nbytes(parts[0].shape, F32),
    )


def final_body(n_exp, chunks, *refs):
    msgs = refs[:n_exp]
    weight_ref, chosen_ref, ids_ref, mine_ref, other_ref = refs[n_exp : n_exp + 5]
    dtok_hbm, dgate_ref, dlat_hbm, out, dlat, sems = refs[n_exp + 5 :]
    dlat[...] = (mine_ref[...].astype(F32) + other_ref[...].astype(F32)).astype(BF16)
    dlat_write = pltpu.make_async_copy(dlat, dlat_hbm, sems.at[chunks])
    dlat_write.start()
    width = msgs[0].shape[1] - LANES
    top, rows = ids_ref.shape
    slots = n_exp * CAP
    weight = weight_ref[...]
    high = weight.astype(BF16)
    rest = weight - high.astype(F32)
    mid = rest.astype(BF16)
    low = (rest - mid.astype(F32)).astype(BF16)
    lhs = jnp.concatenate([high, mid, low], axis=0)
    tn = (((0,), (0,)), ((), ()))
    step = width // chunks
    writes = [dlat_write]
    for c in range(chunks):
        cols = pl.ds(c * step, step)
        piece = jnp.concatenate([msg[:, cols] for msg in msgs], axis=0)
        stacked = jnp.concatenate([piece] * 3, axis=0)
        out[:, cols] = lax.dot_general(lhs, stacked, tn, preferred_element_type=F32).astype(BF16)
        write = pltpu.make_async_copy(out.at[:, cols], dtok_hbm.at[:, cols], sems.at[c])
        write.start()
        writes.append(write)
    tail = jnp.concatenate([msg[:, pl.ds(width, LANES)] for msg in msgs], axis=0)
    kept = chosen_ref[...] * tail[:, :1].astype(F32)
    expert = slot_experts((slots, rows))
    ids = ids_ref[...]
    grads = [
        jnp.sum(jnp.where(ids[j : j + 1] == expert, kept, 0.0), axis=0, keepdims=True)
        for j in range(top)
    ]
    dgate_ref[...] = jnp.concatenate(grads, axis=0).astype(BF16)
    for write in writes:
        write.wait()


def final(msgs, weight, chosen, expert_ids, lat_mine, lat_other):
    n_exp = len(msgs)
    width = msgs[0].shape[1] - LANES
    rows, top = expert_ids.shape
    chunks = 7
    d_tokens, d_gates, d_latent = call(
        functools.partial(final_body, n_exp, chunks),
        [
            jax.ShapeDtypeStruct((rows, width), BF16),
            jax.ShapeDtypeStruct((top, rows), BF16),
            jax.ShapeDtypeStruct(lat_mine.shape, BF16),
        ],
        (*msgs, weight, chosen, expert_ids.T, lat_mine, lat_other),
        [vmem_spec()] * (n_exp + 5),
        [
            pltpu.VMEM((rows, width), BF16),
            pltpu.VMEM(lat_mine.shape, BF16),
            pltpu.SemaphoreType.DMA((chunks + 1,)),
        ],
        12 * MIB,
        flops=6 * n_exp * CAP * rows * width,
        out_specs=[hbm_spec(), vmem_spec(), hbm_spec()],
    )
    return d_tokens, d_gates.T, d_latent


def gather_blocks(own, n_ctx):
    chips = n_ctx // 2
    line = [own] + [chip_exchange(own, p) for p in range(1, chips)]
    return line + [core_exchange(block) for block in line]


def widen_add(*arrays):
    total = arrays[0].astype(F32)
    for array in arrays[1:]:
        total = total + array.astype(F32)
    return total.astype(BF16)


def local(
    queries,
    latent,
    grad_out,
    doc_ids,
    tokens,
    token_grads,
    gate_values,
    expert_ids,
    gate_order,
    w_gate,
    w_up,
    w_down,
):
    n_ctx = lax.axis_size("ctx")
    n_exp = lax.axis_size("exp")
    assert w_gate.shape[0] == 1
    per_dev = latent.shape[0]

    chips = n_ctx // 2
    sends, weight, chosen = route(
        expert_ids, gate_order, gate_values, tokens, token_grads, n_exp
    )
    got = [sends[0]] + [exchange(sends[k], "exp", k) for k in range(1, n_exp)]
    own_rows = jnp.concatenate([g[:CAP] for g in got] + [g[CAP:] for g in got], axis=0)

    doc_cols = jnp.broadcast_to(doc_ids.astype(BF16)[:, None], (per_dev, LANES))
    lat_blocks = gather_blocks(jnp.concatenate([latent, doc_cols], axis=1), n_ctx)
    row_blocks = gather_blocks(own_rows, n_ctx)

    d_queries, lat_even, lat_odd, weights = attention(
        queries, grad_out, lat_blocks, (w_gate, w_up, w_down)
    )
    lat_total = widen_add(lat_even, core_exchange(lat_odd))
    for p in halvings(chips):
        keep, send = lat_total[: p * per_dev], lat_total[p * per_dev :]
        lat_total = widen_add(keep, chip_exchange(send, p))
    mask = 1
    while mask < n_exp:
        if mask > 1:
            lat_total = widen_add(lat_total, lat_other)
        lat_other = exchange(lat_total, "exp", mask)
        mask *= 2

    even, odd = experts(row_blocks, weights)
    summed = pair_sum(even, core_exchange(odd), chips)
    parts = [summed[0]] + [chip_exchange(summed[p], p) for p in range(1, chips)]
    backs = owner_sum(parts, n_exp)
    back = [backs[0]] + [exchange(backs[k], "exp", k) for k in range(1, n_exp)]
    d_tokens, d_gates, d_latent = final(
        back, weight, chosen, expert_ids, lat_total, lat_other
    )
    return (d_queries, d_latent, d_tokens, d_gates)


def solution(mesh):
    in_specs = (
        P("ctx", "exp", None),
        P("ctx", None),
        P("ctx", "exp", None),
        P("ctx"),
        P(("ctx", "exp"), None),
        P(("ctx", "exp"), None),
        P(("ctx", "exp"), None),
        P(("ctx", "exp"), None),
        P(("ctx", "exp"), None),
        P("exp", None, "ctx"),
        P("exp", None, "ctx"),
        P("exp", "ctx", None),
    )
    out_specs = (
        P("ctx", "exp", None),
        P("ctx", None),
        P(("ctx", "exp"), None),
        P(("ctx", "exp"), None),
    )
    return jax.shard_map(local, mesh=mesh, in_specs=in_specs, out_specs=out_specs, check_vma=False)
```

```python
import functools

import jax
import jax.numpy as jnp
from jax import lax
from jax.experimental import pallas as pl
from jax.experimental.pallas import tpu as pltpu
from jax.sharding import PartitionSpec as P


SCALE_DIM = 192
CAP = 2
LANES = 128
MIB = 1 << 20
F32 = jnp.float32
BF16 = jnp.bfloat16


def exchange(array, axis, mask):
    count = lax.axis_size(axis)
    return lax.ppermute(array, axis, [(i, i ^ mask) for i in range(count)])


def turned(place):
    return (place & ~3) | ((place & 1) << 1) | ((place & 2) >> 1)


def chip_exchange(array, place):
    count = lax.axis_size("ctx")
    pairs = [(i, i ^ (2 * (turned(place) if i & 1 else place))) for i in range(count)]
    return lax.ppermute(array, "ctx", pairs)


def core_exchange(array):
    return exchange(array, "ctx", 1)


def vmem_spec():
    return pl.BlockSpec(memory_space=pltpu.VMEM)


def hbm_spec():
    return pl.BlockSpec(memory_space=pltpu.HBM)


def nbytes(shape, dtype):
    total = jnp.dtype(dtype).itemsize
    for size in shape:
        total *= size
    return total


def call(body, outs, args, in_specs, scratch, limit, flops=0, out_specs=None):
    moved = sum(nbytes(a.shape, a.dtype) for a in args)
    moved += sum(nbytes(o.shape, o.dtype) for o in outs)
    args = [
        pltpu.with_memory_space_constraint(a, pltpu.HBM) if s.memory_space == pltpu.HBM else a
        for a, s in zip(args, in_specs)
    ]
    return pl.pallas_call(
        body,
        out_shape=outs,
        in_specs=in_specs,
        out_specs=out_specs or [vmem_spec() for _ in outs],
        scratch_shapes=scratch,
        compiler_params=pltpu.CompilerParams(vmem_limit_bytes=limit),
        cost_estimate=pl.CostEstimate(flops=flops, bytes_accessed=moved, transcendentals=0),
    )(*args)


def halvings(count):
    return [count >> i for i in range(1, count.bit_length())]


def slot_experts(shape):
    slot = lax.broadcasted_iota(jnp.int32, shape, 0)
    return (slot >> (CAP.bit_length() - 1)) ^ lax.axis_index("exp")


def route_body(n_exp, ids_hbm, order_hbm, gates_hbm, tok_hbm, grad_hbm, *rest):
    msgs = rest[:n_exp]
    weight_ref, chosen_ref, ids_ref, order_ref, gates_ref, held, sems = rest[n_exp:]
    pieces = 4
    width = held.shape[2]
    piece = width // pieces
    small = [
        pltpu.make_async_copy(src, dst, sems.at[i])
        for i, (src, dst) in enumerate(
            ((ids_hbm, ids_ref), (order_hbm, order_ref), (gates_hbm, gates_ref))
        )
    ]
    large = [
        pltpu.make_async_copy(
            src.at[:, pl.ds(c * piece, piece)],
            held.at[i, :, pl.ds(c * piece, piece)],
            sems.at[3 + i * pieces + c],
        )
        for c in range(pieces)
        for i, src in enumerate((tok_hbm, grad_hbm))
    ]
    for copy in small + large:
        copy.start()
    for copy in small:
        copy.wait()
    top, rows = ids_ref.shape
    shape = (n_exp * CAP, rows)
    expert = slot_experts(shape)
    ids = ids_ref[...]
    gates = gates_ref[...]
    hits = jnp.zeros(shape, F32)
    mass = jnp.zeros(shape, F32)
    for j in range(top):
        match = ids[j : j + 1] == expert
        hits = hits + jnp.where(match, 1.0, 0.0)
        mass = mass + jnp.where(match, gates[j : j + 1], 0.0)
    order = jnp.broadcast_to(order_ref[...].astype(F32), (rows, rows))
    earlier = jnp.where(order.T < order, 1.0, 0.0).astype(BF16)
    ranks = jnp.dot(hits.astype(BF16), earlier, preferred_element_type=F32)
    slot = (lax.broadcasted_iota(jnp.int32, shape, 0) & (CAP - 1)).astype(F32)
    chosen = jnp.where((hits == 1.0) & (ranks == slot), 1.0, 0.0)
    weight_ref[...] = chosen * mass
    chosen_ref[...] = chosen
    pick = chosen.astype(BF16)
    for c in range(pieces):
        large[2 * c].wait()
        large[2 * c + 1].wait()
        cols = pl.ds(c * piece, piece)
        tok = jnp.dot(pick, held[0, :, cols], preferred_element_type=F32)
        grad = jnp.dot(pick, held[1, :, cols], preferred_element_type=F32)
        for k in range(n_exp):
            span = slice(k * CAP, (k + 1) * CAP)
            msgs[k][:, cols] = jnp.concatenate([tok[span], grad[span]], axis=0).astype(BF16)


def route(expert_ids, gate_order, gate_values, tokens, token_grads, n_exp):
    rows, width = tokens.shape
    top = expert_ids.shape[1]
    outs = [jax.ShapeDtypeStruct((2 * CAP, width), BF16) for _ in range(n_exp)]
    outs += [jax.ShapeDtypeStruct((n_exp * CAP, rows), F32)] * 2
    res = call(
        functools.partial(route_body, n_exp),
        outs,
        (expert_ids.T, gate_order, gate_values.T, tokens, token_grads),
        [hbm_spec()] * 5,
        [
            pltpu.VMEM((top, rows), jnp.int32),
            pltpu.VMEM((1, rows), jnp.int32),
            pltpu.VMEM((top, rows), F32),
            pltpu.VMEM((2, rows, width), BF16),
            pltpu.SemaphoreType.DMA((11,)),
        ],
        12 * MIB,
        flops=4 * n_exp * CAP * rows * width,
    )
    return res[:n_exp], res[n_exp], res[n_exp + 1]


def pack_body(*refs):
    msgs, out = refs[:-1], refs[-1]
    width = out.shape[1]
    step = 1024
    for c in range(width // step):
        cols = pl.ds(c * step, step)
        held = [msg[:, cols].astype(F32) for msg in msgs]
        parts = [h[:CAP] for h in held] + [h[CAP:] for h in held]
        out[:, cols] = jnp.concatenate(parts, axis=0).astype(BF16)


def pack(msgs):
    width = msgs[0].shape[1]
    (rows,) = call(
        pack_body,
        [jax.ShapeDtypeStruct((2 * CAP * len(msgs), width), BF16)],
        tuple(msgs),
        [vmem_spec()] * len(msgs),
        [],
        4 * MIB,
    )
    return rows


def attention_body(n_blocks, heads, row_block, *refs):
    q_ref, go_ref = refs[:2]
    blocks = refs[2 : 2 + n_blocks]
    w_hbm = refs[2 + n_blocks : 5 + n_blocks]
    dq_hbm, even_ref, odd_ref = refs[5 + n_blocks : 8 + n_blocks]
    w_vmem = refs[8 + n_blocks : 11 + n_blocks]
    lat, dq, dq_sems, w_sems = refs[11 + n_blocks :]
    fetches = [
        pltpu.make_async_copy(src.at[0], dst, w_sems.at[i])
        for i, (src, dst) in enumerate(zip(w_hbm, w_vmem))
    ]
    for fetch in fetches:
        fetch.start()
    rows, width = q_ref.shape
    per = rows // heads
    scale = SCALE_DIM ** (-0.5)
    keydoc = []
    at = 0
    for block in blocks:
        lat[at : at + block.shape[0], :] = block[:, :width]
        keydoc.append(block[:, width:].astype(F32))
        at += block.shape[0]
    keydoc = jnp.concatenate(keydoc, axis=0)
    reps = row_block // LANES
    if reps > 1:
        keydoc = jnp.concatenate([keydoc] * reps, axis=1)
    keys = lat[...]
    nt = (((1,), (1,)), ((), ()))
    tn = (((0,), (0,)), ((), ()))
    owner = lax.broadcasted_iota(jnp.int32, (per, row_block), 0)
    col = lax.broadcasted_iota(jnp.int32, (per, row_block), 1)
    acc = None
    writes = []
    for b in range(rows // row_block):
        span = pl.ds(b * row_block, row_block)
        q = q_ref[span, :]
        go = go_ref[span, :]
        at = col + b * row_block
        spread = jnp.where((at >= owner * heads) & (at < (owner + 1) * heads), 1.0, 0.0)
        qdoc = lax.dot_general(
            blocks[0][:per, width:], spread.astype(BF16), tn, preferred_element_type=F32
        )[:1]
        scores = lax.dot_general(keys, q, nt, preferred_element_type=F32) * scale
        scores = jnp.where(keydoc == qdoc, scores, -1e30)
        top = jnp.max(scores, axis=0, keepdims=True)
        probs = jnp.exp(scores - top)
        total = jnp.sum(probs, axis=0, keepdims=True)
        probs = probs * (1.0 / total)
        pgrad = lax.dot_general(keys, go, nt, preferred_element_type=F32)
        delta = jnp.sum(probs * pgrad, axis=0, keepdims=True)
        sgrad = (probs * (pgrad - delta)).astype(BF16)
        probs = probs.astype(BF16)
        dq[span, :] = (
            lax.dot_general(sgrad, keys, tn, preferred_element_type=F32) * scale
        ).astype(BF16)
        write = pltpu.make_async_copy(dq.at[span, :], dq_hbm.at[span, :], dq_sems.at[b])
        write.start()
        writes.append(write)
        term = jnp.dot(sgrad, q, preferred_element_type=F32) * scale
        term = term + jnp.dot(probs, go, preferred_element_type=F32)
        acc = term if acc is None else acc + term
    half = even_ref.shape[0]
    even_ref[...] = acc[:half, :].astype(BF16)
    odd_ref[...] = acc[half:, :].astype(BF16)
    for copy in writes + fetches:
        copy.wait()


def attention(queries, grad_out, blocks, weights):
    n_blocks = len(blocks)
    q_rows, heads, width = queries.shape
    rows = q_rows * heads
    keys = sum(block.shape[0] for block in blocks)
    row_block = min(1024, rows)
    q = queries.reshape(rows, width)
    go = grad_out.reshape(rows, width)
    half = (keys // 2, width)
    outs = [
        jax.ShapeDtypeStruct((rows, width), BF16),
        jax.ShapeDtypeStruct(half, BF16),
        jax.ShapeDtypeStruct(half, BF16),
    ]
    outs += [pltpu.VMEM(w.shape[1:], BF16) for w in weights]
    res = call(
        functools.partial(attention_body, n_blocks, heads, row_block),
        outs,
        (q, go, *blocks, *weights),
        [vmem_spec()] * (2 + n_blocks) + [hbm_spec()] * 3,
        [
            pltpu.VMEM((keys, width), BF16),
            pltpu.VMEM((rows, width), BF16),
            pltpu.SemaphoreType.DMA((rows // row_block,)),
            pltpu.SemaphoreType.DMA((3,)),
        ],
        24 * MIB,
        flops=10 * rows * keys * width,
        out_specs=[hbm_spec()] + [vmem_spec()] * 5,
    )
    return res[0].reshape(queries.shape), res[1], res[2], res[3:]


def split_score(total, lane):
    high = total.astype(BF16).astype(F32)
    low = total - high
    return jnp.where(lane == 0, high, jnp.where(lane == 1, low, 0.0)).astype(BF16)


def expert_body(n_ctx, chunks, *refs):
    blocks = refs[:n_ctx]
    wg, wu, wd, even_ref, odd_ref, xt, xg = refs[n_ctx:]
    hid, width = wd.shape
    step = width // chunks
    per = blocks[0].shape[0] // 2
    for i, block in enumerate(blocks):
        xt[i * per : (i + 1) * per, :] = block[:per, :]
        xg[i * per : (i + 1) * per, :] = block[per:, :]
    rows = per * n_ctx
    nt = (((1,), (1,)), ((), ()))
    gate = jnp.zeros((rows, hid), F32)
    up = jnp.zeros((rows, hid), F32)
    act = jnp.zeros((rows, hid), F32)
    for c in range(chunks):
        cols = pl.ds(c * step, step)
        gate = gate + jnp.dot(xt[:, cols], wg[cols, :], preferred_element_type=F32)
        up = up + jnp.dot(xt[:, cols], wu[cols, :], preferred_element_type=F32)
        act = act + lax.dot_general(xg[:, cols], wd[:, cols], nt, preferred_element_type=F32)
    sig = jax.nn.sigmoid(gate)
    silu = gate * sig
    hidden = (silu * up).astype(BF16).astype(F32)
    score = jnp.sum(hidden * act, axis=1, keepdims=True)
    ggrad = (act * up * sig * (1.0 + gate * (1.0 - sig))).astype(BF16)
    ugrad = (act * silu).astype(BF16)
    half = rows // 2
    lane = lax.broadcasted_iota(jnp.int32, (rows, LANES), 1)
    tail = split_score(score, lane)
    even_ref[:, pl.ds(width, LANES)] = tail[:half]
    odd_ref[:, pl.ds(width, LANES)] = tail[half:]
    fine = 1024
    for c in range(width // fine):
        cols = pl.ds(c * fine, fine)
        part = lax.dot_general(ggrad, wg[cols, :], nt, preferred_element_type=F32)
        part = part + lax.dot_general(ugrad, wu[cols, :], nt, preferred_element_type=F32)
        part = part.astype(BF16)
        even_ref[:, cols] = part[:half]
        odd_ref[:, cols] = part[half:]


def experts(blocks, weights):
    n_ctx = len(blocks)
    width = blocks[0].shape[1]
    hid = weights[0].shape[1]
    rows = blocks[0].shape[0] // 2 * n_ctx
    out = jax.ShapeDtypeStruct((rows // 2, width + LANES), BF16)
    weights = [pltpu.with_memory_space_constraint(w, pltpu.VMEM) for w in weights]
    return call(
        functools.partial(expert_body, n_ctx, 7),
        [out, out],
        (*blocks, *weights),
        [vmem_spec()] * (n_ctx + 3),
        [pltpu.VMEM((rows, width), BF16), pltpu.VMEM((rows, width), BF16)],
        min(30 * MIB, 4 * MIB + 6 * nbytes((rows, width), BF16)),
        flops=10 * rows * width * hid,
    )


def pair_body(n_out, keep_ref, got_ref, *outs):
    width = outs[0].shape[1] - LANES
    per = outs[0].shape[0]
    for i in range(n_out):
        span = pl.ds(i * per, per)
        total = keep_ref[span, :].astype(F32) + got_ref[span, :].astype(F32)
        outs[i][:, :width] = total[:, :width].astype(BF16)
        lane = lax.broadcasted_iota(jnp.int32, (per, LANES), 1)
        score = jnp.sum(total[:, width:], axis=1, keepdims=True)
        outs[i][:, pl.ds(width, LANES)] = split_score(score, lane)


def pair_sum(keep, got, n_out):
    rows, width = keep.shape
    outs = [jax.ShapeDtypeStruct((rows // n_out, width), BF16) for _ in range(n_out)]
    return call(
        functools.partial(pair_body, n_out),
        outs,
        (keep, got),
        [vmem_spec()] * 2,
        [],
        4 * MIB + 6 * nbytes(keep.shape, BF16),
    )


def owner_body(n_in, *refs):
    ins = refs[:n_in]
    outs = refs[n_in:]
    width = ins[0].shape[1] - LANES
    total = ins[0][...].astype(F32)
    for ref in ins[1:]:
        total = total + ref[...].astype(F32)
    score = jnp.sum(total[:, width:], axis=1, keepdims=True)
    lane = lax.broadcasted_iota(jnp.int32, (ins[0].shape[0], LANES), 1)
    tail = jnp.where(lane == 0, score, 0.0)
    for k, out in enumerate(outs):
        span = slice(k * CAP, (k + 1) * CAP)
        out[:, :width] = total[span, :width].astype(BF16)
        out[:, pl.ds(width, LANES)] = tail[span].astype(BF16)


def owner_sum(parts, n_out):
    rows, width = parts[0].shape
    outs = [jax.ShapeDtypeStruct((rows // n_out, width), BF16) for _ in range(n_out)]
    return call(
        functools.partial(owner_body, len(parts)),
        outs,
        tuple(parts),
        [vmem_spec()] * len(parts),
        [],
        4 * MIB + 8 * nbytes(parts[0].shape, F32),
    )


def final_body(n_exp, chunks, *refs):
    msgs = refs[:n_exp]
    weight_ref, chosen_ref, ids_ref, dtok_hbm, dgate_ref, out, sems = refs[n_exp:]
    width = msgs[0].shape[1] - LANES
    top, rows = ids_ref.shape
    slots = n_exp * CAP
    weight = weight_ref[...]
    high = weight.astype(BF16)
    rest = weight - high.astype(F32)
    mid = rest.astype(BF16)
    low = (rest - mid.astype(F32)).astype(BF16)
    lhs = jnp.concatenate([high, mid, low], axis=0)
    tn = (((0,), (0,)), ((), ()))
    step = width // chunks
    writes = []
    for c in range(chunks):
        cols = pl.ds(c * step, step)
        piece = jnp.concatenate([msg[:, cols] for msg in msgs], axis=0)
        stacked = jnp.concatenate([piece] * 3, axis=0)
        out[:, cols] = lax.dot_general(lhs, stacked, tn, preferred_element_type=F32).astype(BF16)
        write = pltpu.make_async_copy(out.at[:, cols], dtok_hbm.at[:, cols], sems.at[c])
        write.start()
        writes.append(write)
    tail = jnp.concatenate([msg[:, pl.ds(width, LANES)] for msg in msgs], axis=0)
    kept = chosen_ref[...] * tail[:, :1].astype(F32)
    expert = slot_experts((slots, rows))
    ids = ids_ref[...]
    grads = [
        jnp.sum(jnp.where(ids[j : j + 1] == expert, kept, 0.0), axis=0, keepdims=True)
        for j in range(top)
    ]
    dgate_ref[...] = jnp.concatenate(grads, axis=0).astype(BF16)
    for write in writes:
        write.wait()


def final(msgs, weight, chosen, expert_ids):
    n_exp = len(msgs)
    width = msgs[0].shape[1] - LANES
    rows, top = expert_ids.shape
    chunks = 7
    d_tokens, d_gates = call(
        functools.partial(final_body, n_exp, chunks),
        [
            jax.ShapeDtypeStruct((rows, width), BF16),
            jax.ShapeDtypeStruct((top, rows), BF16),
        ],
        (*msgs, weight, chosen, expert_ids.T),
        [vmem_spec()] * (n_exp + 3),
        [
            pltpu.VMEM((rows, width), BF16),
            pltpu.SemaphoreType.DMA((chunks,)),
        ],
        12 * MIB,
        flops=6 * n_exp * CAP * rows * width,
        out_specs=[hbm_spec(), vmem_spec()],
    )
    return d_tokens, d_gates.T


def gather_blocks(own, n_ctx):
    chips = n_ctx // 2
    line = [own] + [chip_exchange(own, p) for p in range(1, chips)]
    return line + [core_exchange(block) for block in line]


def widen_add(*arrays):
    total = arrays[0].astype(F32)
    for array in arrays[1:]:
        total = total + array.astype(F32)
    return total.astype(BF16)


def local(
    queries,
    latent,
    grad_out,
    doc_ids,
    tokens,
    token_grads,
    gate_values,
    expert_ids,
    gate_order,
    w_gate,
    w_up,
    w_down,
):
    n_ctx = lax.axis_size("ctx")
    n_exp = lax.axis_size("exp")
    assert w_gate.shape[0] == 1
    per_dev = latent.shape[0]

    chips = n_ctx // 2
    sends, weight, chosen = route(
        expert_ids, gate_order, gate_values, tokens, token_grads, n_exp
    )
    got = [sends[0]] + [exchange(sends[k], "exp", k) for k in range(1, n_exp)]
    own_rows = pack(got)

    doc_cols = jnp.broadcast_to(doc_ids.astype(BF16)[:, None], (per_dev, LANES))
    lat_blocks = gather_blocks(jnp.concatenate([latent, doc_cols], axis=1), n_ctx)
    row_blocks = gather_blocks(own_rows, n_ctx)

    d_queries, lat_even, lat_odd, weights = attention(
        queries, grad_out, lat_blocks, (w_gate, w_up, w_down)
    )
    lat_total = widen_add(lat_even, core_exchange(lat_odd))
    for p in halvings(chips):
        keep, send = lat_total[: p * per_dev], lat_total[p * per_dev :]
        lat_total = widen_add(keep, chip_exchange(send, p))
    mask = 1
    while mask < n_exp:
        if mask > 1:
            lat_total = widen_add(lat_total, lat_other)
        lat_other = exchange(lat_total, "exp", mask)
        mask *= 2

    even, odd = experts(row_blocks, weights)
    summed = pair_sum(even, core_exchange(odd), chips)
    parts = [summed[0]] + [chip_exchange(summed[p], p) for p in range(1, chips)]
    backs = owner_sum(parts, n_exp)
    back = [backs[0]] + [exchange(backs[k], "exp", k) for k in range(1, n_exp)]
    d_tokens, d_gates = final(back, weight, chosen, expert_ids)
    d_latent = widen_add(lat_total, lat_other)
    return (d_queries, d_latent, d_tokens, d_gates)


def solution(mesh):
    in_specs = (
        P("ctx", "exp", None),
        P("ctx", None),
        P("ctx", "exp", None),
        P("ctx"),
        P(("ctx", "exp"), None),
        P(("ctx", "exp"), None),
        P(("ctx", "exp"), None),
        P(("ctx", "exp"), None),
        P(("ctx", "exp"), None),
        P("exp", None, "ctx"),
        P("exp", None, "ctx"),
        P("exp", "ctx", None),
    )
    out_specs = (
        P("ctx", "exp", None),
        P("ctx", None),
        P(("ctx", "exp"), None),
        P(("ctx", "exp"), None),
    )
    return jax.shard_map(local, mesh=mesh, in_specs=in_specs, out_specs=out_specs, check_vma=False)
```
